256 devices in a mesh: outer: 8 (over y, core), inner: 32 (over x, z).
Axes of the slice: x: 4, y: 4, z: 8, core: 2. Of those that a mesh axis runs over, the one named last changes fastest.
Arguments:
- query_rows: bfloat16 [65536, 1024], P(('outer', 'inner')), may hold values from -6 to 6
- key_rows: bfloat16 [65536, 1024], P(('outer', 'inner')), may hold values from -6 to 6
- value_rows: bfloat16 [65536, 1024], P(('outer', 'inner')), may hold values from -6 to 6
- log_decay: float32 [8, 65536], P(None, ('outer', 'inner')), may hold values from -0.8 to 0, as said below
- grad_out: bfloat16 [65536, 1024], P(('outer', 'inner')), may hold values from -6 to 6
Outputs:
- attended: bfloat16 [65536, 1024], P(('outer', 'inner'))
- grad_queries: bfloat16 [65536, 1024], P(('outer', 'inner'))
- grad_keys: bfloat16 [65536, 1024], P(('outer', 'inner'))
- grad_values: bfloat16 [65536, 1024], P(('outer', 'inner'))
The draws below stay inside these ranges and needn't reach their ends.
Inputs may be any that keep to these rules, and one draw needn't show every extreme that they name: `log_decay`: every entry is negative.
All inputs are finite; a program needn't handle non-finite values.
Results may differ from the reference program's by a relative error of at most 0.0063.
Values sent between devices are 32-bit elements; how exact they have to be, the bound alone decides.
No kernel may reach another device: no remote copies, remote signals or barrier semaphores. Data moves between devices by JAX's collectives and lax.ppermute only.
A program may use at most 320 MiB of HBM per device.

```python
import math
import jax
import jax.numpy as jnp
from jax import lax

HALF_HEADS = 8
E = 128
TOK_DEV = 256
SEQUENCE_TOKENS = 65536


def draw_log_decay(key, part):
    random_subkeys = jax.random.split(jax.random.fold_in(key, 17), 7)
    ranking = jax.random.permutation(random_subkeys[0], HALF_HEADS)
    fast_count = HALF_HEADS // 2
    fast_head_flags = ranking < fast_count
    fast_rate = jnp.exp(jax.random.uniform(random_subkeys[1], (HALF_HEADS,), jnp.float32, jnp.log(5.0), jnp.log(50.0))) / SEQUENCE_TOKENS
    slow_rate = jnp.exp(jax.random.uniform(random_subkeys[2], (HALF_HEADS,), jnp.float32, jnp.log(0.05), jnp.log(0.25))) / SEQUENCE_TOKENS
    base_rate = jnp.where(fast_head_flags, fast_rate, slow_rate)
    blocks = SEQUENCE_TOKENS // TOK_DEV
    block_factor = jax.random.uniform(random_subkeys[3], (HALF_HEADS, blocks), jnp.float32, 0.5, 2.0)
    block_factor = jnp.repeat(block_factor, TOK_DEV, axis=1)
    token_factor = jax.random.uniform(random_subkeys[4], (HALF_HEADS, SEQUENCE_TOKENS), jnp.float32, 0.5, 1.5)
    decay_rates = base_rate[:, None] * block_factor * token_factor
    spike_position = jax.random.randint(random_subkeys[5], (HALF_HEADS, 2), 0, SEQUENCE_TOKENS)
    spike_length = jax.random.uniform(random_subkeys[6], (HALF_HEADS, 2), jnp.float32, jnp.log(0.5), jnp.log(0.8))
    token_positions = jnp.arange(SEQUENCE_TOKENS, dtype=jnp.int32)
    spike_flags = token_positions[None, None, :] == spike_position[:, :, None]
    decay_spikes = jnp.sum(jnp.where(spike_flags, spike_length[:, :, None], 0.0), axis=1)
    decay_spikes = jnp.where(fast_head_flags[:, None], 0.0, decay_spikes)
    return (decay_spikes - decay_rates).astype(jnp.float32)


def steps_of(stream_key, shape, cuts, least, largest):
    def one(axis_at, parts):
        draws = jax.random.uniform(jax.random.fold_in(jax.random.fold_in(stream_key, 6), axis_at), (parts,), jnp.float32, least / len(cuts), largest / len(cuts))
        return jnp.repeat(jnp.exp(draws), shape[axis_at] // parts).reshape((-1,) + (1,) * (len(shape) - axis_at - 1))

    factor_of = one(*cuts[0])
    for cut in cuts[1:]:
        factor_of = factor_of * one(*cut)
    return factor_of


def scatter_about(rng, shape, deviation, limit, shards=(), kind=jnp.bfloat16):
    drawn = deviation * jax.random.normal(rng, shape, jnp.float32)
    if shards:
        drawn = drawn * steps_of(rng, shape, shards, -0.22, 0.18)
    return jnp.clip(drawn, -limit, limit).astype(kind)


def setup_inputs(seed: int = 0) -> dict:
    streams_of = jax.random.split(jax.random.key(seed), 6)
    query_rows = scatter_about(streams_of[0], (SEQUENCE_TOKENS, HALF_HEADS * E), 1.0, 6.0, ((0, 256),))
    key_rows = scatter_about(streams_of[1], (SEQUENCE_TOKENS, HALF_HEADS * E), 1.0, 6.0, ((0, 256),))
    value_rows = scatter_about(streams_of[2], (SEQUENCE_TOKENS, HALF_HEADS * E), 1.0, 6.0, ((0, 256),))
    log_decay = draw_log_decay(jax.random.fold_in(streams_of[5], 71), 0)
    grad_out = scatter_about(streams_of[4], (SEQUENCE_TOKENS, HALF_HEADS * E), 1.0, 6.0, ((0, 256),))
    return dict(query_rows=query_rows, key_rows=key_rows, value_rows=value_rows, log_decay=log_decay, grad_out=grad_out)


EPSILON = 1e-06

def causal_decay(running):
    length_rows = running.shape[1]
    row_index = lax.broadcasted_iota(jnp.int32, (length_rows, length_rows), 0)
    col_index = lax.broadcasted_iota(jnp.int32, (length_rows, length_rows), 1)
    causal = (col_index <= row_index)[None]
    gaps = running[:, :, None] - running[:, None, :]
    return jnp.where(causal, jnp.exp(jnp.where(causal, gaps, 0.0)), 0.0)

def block_terms(query_block, key_block, decays, scaling):
    running = jnp.cumsum(decays, axis=1)
    totals = running[:, -1]
    growth = jnp.exp(running).T[:, :, None]
    shrink = jnp.exp(totals[:, None] - running).T[:, :, None]
    query_dec = (query_block.astype(jnp.float32) * growth).astype(jnp.bfloat16)
    key_dec = (key_block.astype(jnp.float32) * shrink).astype(jnp.bfloat16)
    decay_mat = causal_decay(running)
    scores = jnp.einsum('the,she->hts', query_block.astype(jnp.float32), key_block.astype(jnp.float32))
    weights = (scores * scaling * decay_mat).astype(jnp.bfloat16)
    return (totals, growth, shrink, query_dec, key_dec, decay_mat, weights)

def reference(query_rows, key_rows, value_rows, log_decay, grad_out):
    blocks = SEQUENCE_TOKENS // TOK_DEV
    scaling = 1.0 / math.sqrt(E)
    block_shape = (blocks, TOK_DEV, HALF_HEADS, E)
    query_all = query_rows.reshape(block_shape)
    key_all = key_rows.reshape(block_shape)
    value_all = value_rows.reshape(block_shape)
    grad_all = grad_out.reshape(block_shape)
    decay_all = log_decay.reshape(HALF_HEADS, blocks, TOK_DEV).transpose(1, 0, 2)

    def forward_step(carry_state, inputs):
        query_block, key_block, value_block, decays = inputs
        totals, growth, shrink, query_dec, key_dec, decay_mat, weights = block_terms(query_block, key_block, decays, scaling)
        local_state = jnp.einsum('the,thf->hef', key_dec.astype(jnp.float32), value_block.astype(jnp.float32))
        new_state = jnp.exp(totals)[:, None, None] * carry_state + local_state
        return (new_state, carry_state.astype(jnp.bfloat16))
    start_state = jnp.zeros((HALF_HEADS, E, E), jnp.float32)
    _, entering = lax.scan(forward_step, start_state, (query_all, key_all, value_all, decay_all))

    def backward_step(later_state, inputs):
        query_block, key_block, value_block, decays, entering_half, grad_block = inputs
        totals, growth, shrink, query_dec, key_dec, decay_mat, weights = block_terms(query_block, key_block, decays, scaling)
        value_float = value_block.astype(jnp.float32)
        entering_float = entering_half.astype(jnp.float32)
        mixed = jnp.einsum('hts,shf->thf', weights.astype(jnp.float32), value_float)
        mixed = mixed + scaling * jnp.einsum('the,hef->thf', query_dec.astype(jnp.float32), entering_float)
        inverse = lax.rsqrt(lax.optimization_barrier(jnp.mean(mixed * mixed, axis=2, keepdims=True)) + EPSILON)
        normed = mixed * inverse
        grad_normed = grad_block.astype(jnp.float32)
        grad_mixed = (inverse * (grad_normed - normed * lax.optimization_barrier(jnp.mean(grad_normed * normed, axis=2, keepdims=True)))).astype(jnp.bfloat16)
        grad_float = grad_mixed.astype(jnp.float32)
        back_state = scaling * jnp.einsum('the,thf->hef', query_dec.astype(jnp.float32), grad_float)
        leaving_float = later_state.astype(jnp.bfloat16).astype(jnp.float32)
        grad_prob = jnp.einsum('thf,shf->hts', grad_float, value_float)
        grad_score = (grad_prob * scaling * decay_mat).astype(jnp.bfloat16).astype(jnp.float32)
        grad_q = jnp.einsum('hts,she->the', grad_score, key_block.astype(jnp.float32))
        grad_q = grad_q + scaling * growth * jnp.einsum('thf,hef->the', grad_float, entering_float)
        grad_k = jnp.einsum('hts,the->she', grad_score, query_block.astype(jnp.float32))
        grad_k = grad_k + shrink * jnp.einsum('shf,hef->she', value_float, leaving_float)
        grad_v = jnp.einsum('hts,thf->shf', weights.astype(jnp.float32), grad_float)
        grad_v = grad_v + jnp.einsum('she,hef->shf', key_dec.astype(jnp.float32), leaving_float)
        new_later = jnp.exp(totals)[:, None, None] * later_state + back_state
        return (new_later, (normed.astype(jnp.bfloat16), grad_q.astype(jnp.bfloat16), grad_k.astype(jnp.bfloat16), grad_v.astype(jnp.bfloat16)))
    _, results = lax.scan(backward_step, start_state, (query_all, key_all, value_all, decay_all, entering, grad_all), reverse=True)
    attended, grad_queries, grad_keys, grad_values = [piece.reshape(SEQUENCE_TOKENS, HALF_HEADS * E) for piece in results]
    return (attended, grad_queries, grad_keys, grad_values)
```

```python
import math

import jax
import jax.numpy as jnp
from jax import lax
from jax.experimental import pallas as pl
from jax.experimental.pallas import tpu as pltpu
from jax.sharding import Mesh
from jax.sharding import PartitionSpec as P

ALL = ("y", "core", "x", "z")
GROUP = ("x", "z")
EPSILON = 1e-06
HEADS = 8
E = 128
T = 256
PEERS = 32
ROWS = HEADS * E // PEERS
SCALING = 1.0 / math.sqrt(E)
F32 = jnp.float32
BF16 = jnp.bfloat16


def dot(a, b, dims, precision=None):
    return lax.dot_general(a, b, (dims, ((), ())), precision=precision, preferred_element_type=F32)


NN, NT, TN = ((1,), (0,)), ((1,), (1,)), ((0,), (0,))


def lanes(h):
    return slice(h * E, (h + 1) * E)


def causal():
    t = lax.broadcasted_iota(jnp.int32, (T, T), 0)
    s = lax.broadcasted_iota(jnp.int32, (T, T), 1)
    return s <= t


def call(kernel, outs, *args, smem=0, flops=0):
    specs = [pl.BlockSpec(memory_space=pltpu.SMEM)] * smem
    specs += [pl.BlockSpec(memory_space=pltpu.VMEM)] * (len(args) - smem)
    moved = sum(a.size * a.dtype.itemsize for a in args)
    moved += sum(math.prod(s) * jnp.dtype(d).itemsize for s, d in outs)
    return pl.pallas_call(
        kernel,
        out_shape=[jax.ShapeDtypeStruct(s, d) for s, d in outs],
        in_specs=specs,
        out_specs=[pl.BlockSpec(memory_space=pltpu.VMEM)] * len(outs),
        cost_estimate=pl.CostEstimate(flops=flops, bytes_accessed=moved, transcendentals=0),
        compiler_params=pltpu.CompilerParams(vmem_limit_bytes=48 * 1024 * 1024),
    )(*args)


def states_kernel(k_ref, v_ref, decay_ref, sent_ref, run_row_ref, run_col_ref):
    decay = decay_ref[...]
    ones = jnp.where(causal(), 1.0, 0.0).astype(F32)
    run_row = dot(decay, ones, NT, lax.Precision.HIGHEST)
    run_col = dot(ones, decay, NT, lax.Precision.HIGHEST)
    run_row_ref[...] = run_row
    run_col_ref[...] = run_col
    shrink = jnp.exp(run_col[T - 1 : T, :] - run_col)
    totals = jnp.broadcast_to(run_row[:, T - 1 : T], (HEADS, E))
    per_head = E // ROWS
    for h in range(HEADS):
        key_dec = (k_ref[:, lanes(h)].astype(F32) * shrink[:, h : h + 1]).astype(BF16)
        state = dot(key_dec, v_ref[:, lanes(h)], TN)
        for i in range(per_head):
            sent_ref[h * per_head + i, :ROWS, :] = state[i * ROWS : (i + 1) * ROWS]
    for r in range(PEERS):
        sent_ref[r, ROWS:, :] = totals


def local_kernel(q_ref, k_ref, v_ref, run_row_ref, run_col_ref, weights_ref, mixed_ref, query_dec_ref):
    mask = causal()
    growth = jnp.exp(run_col_ref[...])
    for h in range(HEADS):
        q = q_ref[:, lanes(h)]
        gap = run_col_ref[:, h : h + 1] - run_row_ref[h : h + 1, :]
        decay = jnp.exp(jnp.where(mask, gap, -1e30))
        scores = dot(q, k_ref[:, lanes(h)], NT)
        weights = (scores * SCALING * decay).astype(BF16)
        weights_ref[h] = weights
        mixed_ref[:, lanes(h)] = dot(weights, v_ref[:, lanes(h)], NN)
        query_dec_ref[:, lanes(h)] = (q.astype(F32) * growth[:, h : h + 1]).astype(BF16)


def mixed_kernel(mixed_ref, query_dec_ref, g_ref, entering_ref, attended_ref, grad_mixed_ref, state_ref):
    for h in range(HEADS):
        query_dec = query_dec_ref[:, lanes(h)]
        mixed = mixed_ref[:, lanes(h)] + SCALING * dot(query_dec, entering_ref[h].astype(BF16), NN)
        inverse = lax.rsqrt(jnp.mean(mixed * mixed, axis=1, keepdims=True) + EPSILON)
        normed = mixed * inverse
        attended_ref[:, lanes(h)] = normed.astype(BF16)
        g = g_ref[:, lanes(h)].astype(F32)
        grad_mixed = inverse * (g - normed * jnp.mean(g * normed, axis=1, keepdims=True))
        grad_mixed = grad_mixed.astype(BF16)
        grad_mixed_ref[:, lanes(h)] = grad_mixed
        state_ref[h] = SCALING * dot(query_dec, grad_mixed, TN)


def local_grads_kernel(
    q_ref, k_ref, v_ref, run_row_ref, run_col_ref, weights_ref, grad_mixed_ref, entering_ref,
    grad_q_ref, grad_k_ref, grad_v_ref,
):
    mask = causal()
    growth = jnp.exp(run_col_ref[...]) * SCALING
    for h in range(HEADS):
        grad_mixed = grad_mixed_ref[:, lanes(h)]
        gap = run_col_ref[:, h : h + 1] - run_row_ref[h : h + 1, :]
        decay = jnp.exp(jnp.where(mask, gap, -1e30))
        grad_prob = dot(grad_mixed, v_ref[:, lanes(h)], NT)
        grad_score = (grad_prob * SCALING * decay).astype(BF16)
        grad_q = dot(grad_score, k_ref[:, lanes(h)], NN)
        grad_q = grad_q + growth[:, h : h + 1] * dot(grad_mixed, entering_ref[h].astype(BF16), NT)
        grad_q_ref[:, lanes(h)] = grad_q.astype(BF16)
        grad_k_ref[:, lanes(h)] = dot(grad_score, q_ref[:, lanes(h)], TN)
        grad_v_ref[:, lanes(h)] = dot(weights_ref[h], grad_mixed, TN)


def final_kernel(k_ref, v_ref, run_col_ref, part_k_ref, part_v_ref, leaving_ref, grad_k_ref, grad_v_ref):
    run_col = run_col_ref[...]
    shrink = jnp.exp(run_col[T - 1 : T, :] - run_col)
    for h in range(HEADS):
        leaving = leaving_ref[h].astype(BF16)
        column = shrink[:, h : h + 1]
        key_dec = (k_ref[:, lanes(h)].astype(F32) * column).astype(BF16)
        grad_k = part_k_ref[:, lanes(h)] + column * dot(v_ref[:, lanes(h)], leaving, NT)
        grad_v = part_v_ref[:, lanes(h)] + dot(key_dec, leaving, NN)
        grad_k_ref[:, lanes(h)] = grad_k.astype(BF16)
        grad_v_ref[:, lanes(h)] = grad_v.astype(BF16)


def group_total_kernel(place_ref, recv_ref, total_ref, decays_ref):
    head = place_ref[0]
    total = recv_ref[0, :ROWS, :]
    logs = recv_ref[0, pl.ds(ROWS + head, 1), :]
    decays_ref[0:1, :] = jnp.exp(logs)
    for j in range(1, PEERS):
        log = recv_ref[j, pl.ds(ROWS + head, 1), :]
        decay = jnp.exp(log)
        decays_ref[j : j + 1, :] = decay
        total = decay * total + recv_ref[j, :ROWS, :]
        logs = logs + log
    total_ref[:ROWS, :] = total
    total_ref[ROWS:, :] = jnp.broadcast_to(logs, (8, E))


def back_total_kernel(recv_ref, decays_ref, total_ref):
    total = recv_ref[PEERS - 1]
    for j in reversed(range(PEERS - 1)):
        total = decays_ref[j : j + 1, :] * total + recv_ref[j]
    total_ref[...] = total


def spread_kernel(reverse, rows_of, place_ref, recv_ref, decays_ref, far_ref, far_decay_ref, out_ref):
    state = jnp.zeros((ROWS, E), F32)
    for i in range(4):
        counts = place_ref[1 + i] > 0
        stepped = far_decay_ref[i : i + 1, :] * state + far_ref[i, :ROWS, :]
        state = jnp.where(counts, stepped, state)
    for j in reversed(range(PEERS)) if reverse else range(PEERS):
        out_ref[j] = state
        state = decays_ref[j : j + 1, :] * state + recv_ref[j, :ROWS, :]


def shifted(array, by):
    size = 4
    return lax.ppermute(array, "y", [(i, (i + by) % size) for i in range(size)])


def swapped(array):
    return lax.ppermute(array, "core", [(0, 1), (1, 0)])


def exchanged(array):
    return lax.all_to_all(array, GROUP, 0, 0, tiled=True)


def body(q, k, v, log_decay, g):
    y, core = lax.axis_index("y"), lax.axis_index("core")
    head = (lax.axis_index("x") * 8 + lax.axis_index("z")) // (PEERS // HEADS)
    wide = (T, HEADS * E)

    sent, run_row, run_col = call(
        states_kernel, [((PEERS, ROWS + 8, E), F32), ((HEADS, T), F32), ((T, HEADS), F32)],
        k, v, log_decay, flops=2 * HEADS * T * E * E,
    )
    recv = exchanged(sent)
    weights, mixed_part, query_dec = call(
        local_kernel, [((HEADS, T, T), BF16), (wide, F32), (wide, BF16)],
        q, k, v, run_row, run_col, flops=4 * HEADS * T * T * E,
    )
    fold = jnp.stack([head]).astype(jnp.int32)
    total, decays = call(
        group_total_kernel, [((ROWS + 8, E), F32), ((PEERS, E), F32)], fold, recv, smem=1,
    )
    other = swapped(total)
    log_mine, log_other = total[ROWS : ROWS + 1], other[ROWS : ROWS + 1]
    decay_mine, decay_other = jnp.exp(log_mine), jnp.exp(log_other)
    both = jnp.where(core == 0, decay_other * total[:ROWS] + other[:ROWS], decay_mine * other[:ROWS] + total[:ROWS])
    both = jnp.concatenate([both, jnp.broadcast_to(log_mine + log_other, (8, E))])
    near = [shifted(both, by) for by in (3, 2, 1)]
    far = jnp.stack([n[:ROWS] for n in near] + [other[:ROWS]])
    far_decay = jnp.exp(jnp.concatenate([n[ROWS : ROWS + 1] for n in near] + [log_other]))
    flags = [head, y >= 3, y >= 2, y >= 1, core == 1]
    place = jnp.stack([jnp.asarray(f).astype(jnp.int32) for f in flags])
    entering_sent = call(
        lambda *refs: spread_kernel(False, ROWS + 8, *refs), [((PEERS, ROWS, E), F32)],
        place, recv, decays, far, far_decay, smem=1,
    )[0]
    entering = exchanged(entering_sent).reshape(HEADS, E, E)

    attended, grad_mixed, state = call(
        mixed_kernel, [(wide, BF16), (wide, BF16), ((HEADS, E, E), F32)],
        mixed_part, query_dec, g, entering, flops=4 * HEADS * T * E * E,
    )
    recv = exchanged(state.reshape(PEERS, ROWS, E))
    grad_q, part_k, part_v = call(
        local_grads_kernel, [(wide, BF16), (wide, F32), (wide, F32)],
        q, k, v, run_row, run_col, weights, grad_mixed, entering, flops=9 * HEADS * T * T * E,
    )
    total = call(back_total_kernel, [((ROWS, E), F32)], recv, decays)[0]
    other = swapped(total)
    both = jnp.where(core == 0, decay_mine * other + total, decay_other * total + other)
    near = [shifted(both, -by) for by in (3, 2, 1)]
    far = jnp.stack(near + [other])
    far_decay = jnp.stack([far_decay[2], far_decay[1], far_decay[0], far_decay[3]])
    flags = [head, y <= 0, y <= 1, y <= 2, core == 0]
    place = jnp.stack([jnp.asarray(f).astype(jnp.int32) for f in flags])
    leaving_sent = call(
        lambda *refs: spread_kernel(True, ROWS, *refs), [((PEERS, ROWS, E), F32)],
        place, recv, decays, far, far_decay, smem=1,
    )[0]
    leaving = exchanged(leaving_sent).reshape(HEADS, E, E)
    grad_k, grad_v = call(
        final_kernel, [(wide, BF16), (wide, BF16)],
        k, v, run_col, part_k, part_v, leaving, flops=4 * HEADS * T * E * E,
    )
    return attended, grad_q, grad_k, grad_v


def solution(mesh):
    finer = Mesh(mesh.devices.reshape(4, 2, 4, 8), ALL)
    rows = P(ALL, None)
    return jax.shard_map(
        body,
        mesh=finer,
        in_specs=(rows, rows, rows, P(None, ALL), rows),
        out_specs=(rows, rows, rows, rows),
        check_vma=False,
    )
```

```python
import math

import jax
import jax.numpy as jnp
from jax import lax
from jax.experimental import pallas as pl
from jax.experimental.pallas import tpu as pltpu
from jax.sharding import Mesh
from jax.sharding import PartitionSpec as P

ALL = ("y", "core", "x", "z")
GROUP = ("x", "z")
EPSILON = 1e-06
HEADS = 8
E = 128
T = 256
PEERS = 32
ROWS = HEADS * E // PEERS
PER_HEAD = PEERS // HEADS
SPAN = ROWS + 1
PIECES = 4
SCALING = 1.0 / math.sqrt(E)
F32 = jnp.float32
BF16 = jnp.bfloat16


def dot(a, b, dims, precision=None):
    return lax.dot_general(a, b, (dims, ((), ())), precision=precision, preferred_element_type=F32)


NN, NT, TN = ((1,), (0,)), ((1,), (1,)), ((0,), (0,))


def lanes(h):
    return slice(h * E, (h + 1) * E)


def causal():
    t = lax.broadcasted_iota(jnp.int32, (T, T), 0)
    s = lax.broadcasted_iota(jnp.int32, (T, T), 1)
    return s <= t


def call(kernel, outs, *args, smem=0, flops=0, hbm_in=(), hbm_out=(), scratch=(), grant=12):
    def spec(space):
        return pl.BlockSpec(memory_space=space)

    ins = [spec(pltpu.SMEM if i < smem else pltpu.HBM if i in hbm_in else pltpu.VMEM) for i in range(len(args))]
    moved = sum(a.size * a.dtype.itemsize for a in args)
    moved += sum(math.prod(s) * jnp.dtype(d).itemsize for s, d in outs)
    return pl.pallas_call(
        kernel,
        out_shape=[pltpu.HBM(s, d) if i in hbm_out else jax.ShapeDtypeStruct(s, d) for i, (s, d) in enumerate(outs)],
        in_specs=ins,
        out_specs=[spec(pltpu.HBM if i in hbm_out else pltpu.VMEM) for i in range(len(outs))],
        scratch_shapes=scratch,
        cost_estimate=pl.CostEstimate(flops=flops, bytes_accessed=moved, transcendentals=0),
        compiler_params=pltpu.CompilerParams(vmem_limit_bytes=grant * 1024 * 1024),
    )(*[pltpu.with_memory_space_constraint(a, pltpu.HBM) if i in hbm_in else a for i, a in enumerate(args)])


def pieces(source, target, sems, count=PIECES):
    size = source.shape[0] // count
    return [
        pltpu.make_async_copy(source.at[pl.ds(i * size, size)], target.at[pl.ds(i * size, size)], sems.at[i])
        for i in range(count)
    ]


def start(copies):
    for copy in copies:
        copy.start()


def wait(copies):
    for copy in copies:
        copy.wait()


def half_copies(pairs, half, wide):
    copies = []
    for source, target, sem in pairs:
        if wide:
            here = pl.ds(half * HEADS * E // 2, HEADS * E // 2)
            copies.append(pltpu.make_async_copy(source.at[:, here], target.at[:, here], sem.at[half]))
        else:
            size = source.shape[0] // 2
            here = pl.ds(half * size, size)
            copies.append(pltpu.make_async_copy(source.at[here], target.at[here], sem.at[half]))
    return copies


def states_kernel(
    k_hbm, v_hbm, decay_hbm, sent_hbm, run_row_hbm, run_col_hbm,
    k_ref, v_ref, decay_ref, sent_ref, run_row_ref, run_col_ref, k_sem, v_sem, out_sem, small_sem,
):
    load_decay = pltpu.make_async_copy(decay_hbm, decay_ref, small_sem.at[0])
    loads = pieces(k_hbm, k_ref, k_sem) + pieces(v_hbm, v_ref, v_sem)
    load_decay.start()
    start(loads)
    ones = jnp.where(causal(), 1.0, 0.0).astype(F32)
    load_decay.wait()
    decay = decay_ref[...]
    run_row = dot(decay, ones, NT, lax.Precision.HIGHEST)
    run_col = dot(ones, decay, NT, lax.Precision.HIGHEST)
    run_row_ref[...] = run_row
    run_col_ref[...] = run_col
    totals = jnp.broadcast_to(run_row[:, T - 1 : T], (HEADS, E))
    small = [
        pltpu.make_async_copy(run_row_ref, run_row_hbm, small_sem.at[1]),
        pltpu.make_async_copy(run_col_ref, run_col_hbm, small_sem.at[2]),
    ]
    start(small)
    shrink = jnp.exp(run_col[T - 1 : T, :] - run_col)
    wait(loads)
    for half in range(2):
        for h in range(half * HEADS // 2, (half + 1) * HEADS // 2):
            key_dec = (k_ref[:, lanes(h)].astype(F32) * shrink[:, h : h + 1]).astype(BF16)
            state = dot(key_dec, v_ref[:, lanes(h)], TN)
            for i in range(PER_HEAD):
                row = (h * PER_HEAD + i) * SPAN
                sent_ref[row : row + ROWS] = state[i * ROWS : (i + 1) * ROWS]
                sent_ref[row + ROWS : row + SPAN] = totals[h : h + 1]
        start(half_copies([(sent_ref, sent_hbm, out_sem)], half, False))
    wait(small)
    for half in range(2):
        wait(half_copies([(sent_ref, sent_hbm, out_sem)], half, False))


def local_kernel(
    q_hbm, k_hbm, v_hbm, run_row_ref, run_col_ref, weights_hbm, mixed_ref, query_dec_ref,
    q_ref, k_ref, v_ref, weights_ref, q_sem, k_sem, v_sem, out_sem,
):
    loads = pieces(q_hbm, q_ref, q_sem) + pieces(k_hbm, k_ref, k_sem) + pieces(v_hbm, v_ref, v_sem)
    start(loads)
    mask = causal()
    growth = jnp.exp(run_col_ref[...])
    wait(loads)
    for h in range(HEADS):
        q = q_ref[:, lanes(h)]
        gap = run_col_ref[:, h : h + 1] - run_row_ref[h : h + 1, :]
        decay = jnp.exp(jnp.where(mask, gap, -1e30))
        scores = dot(q, k_ref[:, lanes(h)], NT)
        weights = (scores * SCALING * decay).astype(BF16)
        weights_ref[h] = weights
        mixed_ref[:, lanes(h)] = dot(weights, v_ref[:, lanes(h)], NN)
        query_dec_ref[:, lanes(h)] = (q.astype(F32) * growth[:, h : h + 1]).astype(BF16)
    stores = pieces(weights_ref, weights_hbm, out_sem)
    start(stores)
    wait(stores)


def mixed_kernel(
    mixed_ref, query_dec_ref, g_ref, entering_ref, attended_hbm, grad_mixed_hbm, state_hbm, half_hbm,
    attended_ref, grad_mixed_ref, state_ref, half_ref, attended_sem, grad_mixed_sem, state_sem, half_sem,
):
    def send(half):
        tall = [(state_ref, state_hbm, state_sem), (half_ref, half_hbm, half_sem)]
        wide = [(attended_ref, attended_hbm, attended_sem), (grad_mixed_ref, grad_mixed_hbm, grad_mixed_sem)]
        return half_copies(tall, half, False) + half_copies(wide, half, True)

    for half in range(2):
        for h in range(half * HEADS // 2, (half + 1) * HEADS // 2):
            query_dec = query_dec_ref[:, lanes(h)]
            entering = entering_ref[h].astype(BF16)
            half_ref[h] = entering
            mixed = mixed_ref[:, lanes(h)] + SCALING * dot(query_dec, entering, NN)
            inverse = lax.rsqrt(jnp.mean(mixed * mixed, axis=1, keepdims=True) + EPSILON)
            normed = mixed * inverse
            attended_ref[:, lanes(h)] = normed.astype(BF16)
            g = g_ref[:, lanes(h)].astype(F32)
            grad_mixed = inverse * (g - normed * jnp.mean(g * normed, axis=1, keepdims=True))
            grad_mixed = grad_mixed.astype(BF16)
            grad_mixed_ref[:, lanes(h)] = grad_mixed
            state_ref[h] = SCALING * dot(query_dec, grad_mixed, TN)
        start(send(half))
    for half in range(2):
        wait(send(half))


def local_grads_kernel(
    q_hbm, k_hbm, v_hbm, weights_hbm, run_row_ref, run_col_ref, grad_mixed_ref, half_ref,
    grad_q_hbm, part_k_ref, part_v_ref,
    q_ref, k_ref, v_ref, weights_ref, grad_q_ref, q_sem, k_sem, v_sem, w_sem, out_sem,
):
    loads = pieces(q_hbm, q_ref, q_sem) + pieces(k_hbm, k_ref, k_sem)
    loads += pieces(v_hbm, v_ref, v_sem) + pieces(weights_hbm, weights_ref, w_sem)
    start(loads)
    mask = causal()
    growth = jnp.exp(run_col_ref[...]) * SCALING
    wait(loads)
    for h in range(HEADS):
        grad_mixed = grad_mixed_ref[:, lanes(h)]
        gap = run_col_ref[:, h : h + 1] - run_row_ref[h : h + 1, :]
        decay = jnp.exp(jnp.where(mask, gap, -1e30))
        grad_prob = dot(grad_mixed, v_ref[:, lanes(h)], NT)
        grad_score = (grad_prob * SCALING * decay).astype(BF16)
        grad_q = dot(grad_score, k_ref[:, lanes(h)], NN)
        grad_q = grad_q + growth[:, h : h + 1] * dot(grad_mixed, half_ref[h], NT)
        grad_q_ref[:, lanes(h)] = grad_q.astype(BF16)
        part_k_ref[:, lanes(h)] = dot(grad_score, q_ref[:, lanes(h)], TN)
        part_v_ref[:, lanes(h)] = dot(weights_ref[h], grad_mixed, TN)
    stores = pieces(grad_q_ref, grad_q_hbm, out_sem)
    start(stores)
    wait(stores)


def final_kernel(
    k_ref, v_ref, run_col_ref, part_k_ref, part_v_hbm, leaving_ref, grad_k_hbm, grad_v_hbm,
    part_v_ref, grad_k_ref, grad_v_ref, in_sem, k_sem, v_sem,
):
    loads = pieces(part_v_hbm, part_v_ref, in_sem)
    start(loads)
    run_col = run_col_ref[...]
    shrink = jnp.exp(run_col[T - 1 : T, :] - run_col)
    for h in range(HEADS):
        grad_k = shrink[:, h : h + 1] * dot(v_ref[:, lanes(h)], leaving_ref[h].astype(BF16), NT)
        grad_k_ref[:, lanes(h)] = (part_k_ref[:, lanes(h)] + grad_k).astype(BF16)
    store_k = pieces(grad_k_ref, grad_k_hbm, k_sem)
    start(store_k)
    wait(loads)
    for h in range(HEADS):
        key_dec = (k_ref[:, lanes(h)].astype(F32) * shrink[:, h : h + 1]).astype(BF16)
        grad_v = dot(key_dec, leaving_ref[h].astype(BF16), NN)
        grad_v_ref[:, lanes(h)] = (part_v_ref[:, lanes(h)] + grad_v).astype(BF16)
    store_v = pieces(grad_v_ref, grad_v_hbm, v_sem)
    start(store_v)
    wait(store_k + store_v)


def group_total_kernel(recv_ref, total_ref, decays_ref):
    total = recv_ref[:ROWS]
    logs = recv_ref[ROWS:SPAN]
    decays_ref[0:1, :] = jnp.exp(logs)
    for j in range(1, PEERS):
        log = recv_ref[j * SPAN + ROWS : (j + 1) * SPAN]
        decay = jnp.exp(log)
        decays_ref[j : j + 1, :] = decay
        total = decay * total + recv_ref[j * SPAN : j * SPAN + ROWS]
        logs = logs + log
    total_ref[:ROWS, :] = total
    total_ref[ROWS:, :] = jnp.broadcast_to(jnp.exp(logs), (8, E))


def back_total_kernel(recv_ref, decays_ref, total_ref):
    total = recv_ref[(PEERS - 1) * ROWS :]
    for j in reversed(range(PEERS - 1)):
        total = decays_ref[j : j + 1, :] * total + recv_ref[j * ROWS : (j + 1) * ROWS]
    total_ref[...] = total


def both_kernel(reverse, place_ref, mine_ref, other_ref, decay_mine_ref, decay_other_ref, both_ref):
    mine, other = mine_ref[:ROWS, :], other_ref[:ROWS, :]
    decay_mine, decay_other = decay_mine_ref[ROWS : ROWS + 1, :], decay_other_ref[ROWS : ROWS + 1, :]
    mine_last = (place_ref[1] == 0) if reverse else (place_ref[1] == 1)
    both = jnp.where(mine_last, decay_mine * other + mine, decay_other * mine + other)
    both_ref[:ROWS, :] = both
    if not reverse:
        both_ref[ROWS:, :] = jnp.broadcast_to(decay_mine * decay_other, (8, E))


def spread_kernel(
    reverse, place_ref, recv_ref, decays_ref, far3_ref, far2_ref, far1_ref, other_ref,
    decay3_ref, decay2_ref, decay1_ref, decay_other_ref, out_ref,
):
    y, core = place_ref[0], place_ref[1]
    span = recv_ref.shape[0] // PEERS
    state = jnp.zeros((ROWS, E), F32)
    steps = [(far3_ref, decay3_ref, 3), (far2_ref, decay2_ref, 2), (far1_ref, decay1_ref, 1)]
    for far_ref, decay_ref, by in steps:
        counts = (y + by < 4) if reverse else (y >= by)
        stepped = decay_ref[ROWS : ROWS + 1, :] * state + far_ref[:ROWS, :]
        state = jnp.where(counts, stepped, state)
    counts = (core == 0) if reverse else (core == 1)
    state = jnp.where(counts, decay_other_ref[ROWS : ROWS + 1, :] * state + other_ref[:ROWS, :], state)
    for j in reversed(range(PEERS)) if reverse else range(PEERS):
        out_ref[j] = state
        state = decays_ref[j : j + 1, :] * state + recv_ref[j * span : j * span + ROWS]


def shifted(array, by):
    return lax.ppermute(array, "y", [(i, (i + by) % 4) for i in range(4)])


def swapped(array):
    return lax.ppermute(array, "core", [(0, 1), (1, 0)])


def exchanged(array):
    return lax.all_to_all(array, GROUP, 0, 0, tiled=True)


def both_of(reverse, rows, place, *args):
    return call(lambda *refs: both_kernel(reverse, *refs), [((rows, E), F32)], place, *args, smem=1)[0]


def spread(reverse, place, *args):
    return call(lambda *refs: spread_kernel(reverse, *refs), [((PEERS, ROWS, E), F32)], place, *args, smem=1)[0]


def body(q, k, v, log_decay, g):
    y, core = lax.axis_index("y"), lax.axis_index("core")
    place = jnp.stack([y, core]).astype(jnp.int32)
    wide = (T, HEADS * E)
    narrow = pltpu.VMEM(wide, BF16)
    square = pltpu.VMEM((HEADS, T, T), BF16)
    sems, two = pltpu.SemaphoreType.DMA((PIECES,)), pltpu.SemaphoreType.DMA((2,))

    sent, run_row, run_col = call(
        states_kernel, [((PEERS * SPAN, E), F32), ((HEADS, T), F32), ((T, HEADS), F32)],
        k, v, log_decay, flops=2 * HEADS * T * E * E, grant=60, hbm_in=(0, 1, 2), hbm_out=(0, 1, 2),
        scratch=[
            narrow, narrow, pltpu.VMEM((HEADS, T), F32), pltpu.VMEM((PEERS * SPAN, E), F32),
            pltpu.VMEM((HEADS, T), F32), pltpu.VMEM((T, HEADS), F32), sems, sems, two, sems,
        ],
    )
    recv = exchanged(sent.reshape(PEERS, 1, SPAN * E)).reshape(PEERS * SPAN, E)
    weights, mixed_part, query_dec = call(
        local_kernel, [((HEADS, T, T), BF16), (wide, F32), (wide, BF16)],
        q, k, v, run_row, run_col, flops=4 * HEADS * T * T * E, grant=60, hbm_in=(0, 1, 2), hbm_out=(0,),
        scratch=[narrow, narrow, narrow, square, sems, sems, sems, sems],
    )
    recv, mixed_part, query_dec = lax.optimization_barrier((recv, mixed_part, query_dec))
    total, decays = call(
        group_total_kernel, [((ROWS + 8, E), F32), ((PEERS, E), F32)], recv,
    )
    other = swapped(total)
    both = both_of(False, ROWS + 8, place, total, other, total, other)
    far3, far2, far1 = [shifted(both, by) for by in (3, 2, 1)]
    entering = exchanged(spread(False, place, recv, decays, far3, far2, far1, other, far3, far2, far1, other))
    entering = entering.reshape(HEADS, E, E)

    attended, grad_mixed, state, half = call(
        mixed_kernel, [(wide, BF16), (wide, BF16), ((HEADS, E, E), F32), ((HEADS, E, E), BF16)],
        mixed_part, query_dec, g, entering, flops=4 * HEADS * T * E * E, hbm_out=(0, 1, 2, 3),
        scratch=[narrow, narrow, pltpu.VMEM((HEADS, E, E), F32), pltpu.VMEM((HEADS, E, E), BF16), two, two, two, two],
    )
    recv = exchanged(state.reshape(PEERS, ROWS, E)).reshape(PEERS * ROWS, E)
    grad_q, part_k, part_v = call(
        local_grads_kernel, [(wide, BF16), (wide, F32), (wide, F32)],
        q, k, v, weights, run_row, run_col, grad_mixed, half, flops=9 * HEADS * T * T * E,
        grant=56, hbm_in=(0, 1, 2, 3), hbm_out=(0,),
        scratch=[narrow, narrow, narrow, square, narrow, sems, sems, sems, sems, sems],
    )
    recv, part_k, part_v = lax.optimization_barrier((recv, part_k, part_v))
    back_total = call(back_total_kernel, [((ROWS, E), F32)], recv, decays)[0]
    back_other = swapped(back_total)
    back_both = both_of(True, ROWS, place, back_total, back_other, total, other)
    back3, back2, back1 = [shifted(back_both, -by) for by in (3, 2, 1)]
    leaving = exchanged(spread(True, place, recv, decays, back3, back2, back1, back_other, far1, far2, far3, other))
    leaving = leaving.reshape(HEADS, E, E)
    grad_k, grad_v = call(
        final_kernel, [(wide, BF16), (wide, BF16)],
        k, v, run_col, part_k, part_v, leaving, flops=4 * HEADS * T * E * E, hbm_in=(4,), hbm_out=(0, 1),
        scratch=[pltpu.VMEM(wide, F32), narrow, narrow, sems, sems, sems],
    )
    return attended, grad_q, grad_k, grad_v


def solution(mesh):
    finer = Mesh(mesh.devices.reshape(4, 2, 4, 8), ALL)
    rows = P(ALL, None)
    return jax.shard_map(
        body,
        mesh=finer,
        in_specs=(rows, rows, rows, P(None, ALL), rows),
        out_specs=(rows, rows, rows, rows),
        check_vma=False,
    )
```

```python
import math

import jax
import jax.numpy as jnp
from jax import lax
from jax.experimental import pallas as pl
from jax.experimental.pallas import tpu as pltpu
from jax.sharding import Mesh
from jax.sharding import PartitionSpec as P

ALL = ("y", "core", "x", "z")
GROUP = ("x", "z")
EPSILON = 1e-06
HEADS = 8
E = 128
T = 256
PEERS = 32
ROWS = HEADS * E // PEERS
PER_HEAD = PEERS // HEADS
SPAN = ROWS + 1
PIECES = 4
SCALING = 1.0 / math.sqrt(E)
F32 = jnp.float32
BF16 = jnp.bfloat16


def dot(a, b, dims, precision=None):
    return lax.dot_general(a, b, (dims, ((), ())), precision=precision, preferred_element_type=F32)


NN, NT, TN = ((1,), (0,)), ((1,), (1,)), ((0,), (0,))


def lanes(h):
    return slice(h * E, (h + 1) * E)


def causal():
    t = lax.broadcasted_iota(jnp.int32, (T, T), 0)
    s = lax.broadcasted_iota(jnp.int32, (T, T), 1)
    return s <= t


def call(kernel, outs, *args, smem=0, flops=0, hbm_in=(), hbm_out=(), scratch=(), grant=16):
    def spec(space):
        return pl.BlockSpec(memory_space=space)

    ins = [spec(pltpu.SMEM if i < smem else pltpu.HBM if i in hbm_in else pltpu.VMEM) for i in range(len(args))]
    moved = sum(a.size * a.dtype.itemsize for a in args)
    moved += sum(math.prod(s) * jnp.dtype(d).itemsize for s, d in outs)
    return pl.pallas_call(
        kernel,
        out_shape=[pltpu.HBM(s, d) if i in hbm_out else jax.ShapeDtypeStruct(s, d) for i, (s, d) in enumerate(outs)],
        in_specs=ins,
        out_specs=[spec(pltpu.HBM if i in hbm_out else pltpu.VMEM) for i in range(len(outs))],
        scratch_shapes=scratch,
        cost_estimate=pl.CostEstimate(flops=flops, bytes_accessed=moved, transcendentals=0),
        compiler_params=pltpu.CompilerParams(vmem_limit_bytes=grant * 1024 * 1024),
    )(*[pltpu.with_memory_space_constraint(a, pltpu.HBM) if i in hbm_in else a for i, a in enumerate(args)])


def pieces(source, target, sems, count=PIECES):
    size = source.shape[0] // count
    return [
        pltpu.make_async_copy(source.at[pl.ds(i * size, size)], target.at[pl.ds(i * size, size)], sems.at[i])
        for i in range(count)
    ]


def start(copies):
    for copy in copies:
        copy.start()


def wait(copies):
    for copy in copies:
        copy.wait()


def half_copies(pairs, half, wide):
    copies = []
    for source, target, sem in pairs:
        if wide:
            here = pl.ds(half * HEADS * E // 2, HEADS * E // 2)
            copies.append(pltpu.make_async_copy(source.at[:, here], target.at[:, here], sem.at[half]))
        else:
            size = source.shape[0] // 2
            here = pl.ds(half * size, size)
            copies.append(pltpu.make_async_copy(source.at[here], target.at[here], sem.at[half]))
    return copies


def states_kernel(
    k_hbm, v_hbm, decay_hbm, sent_hbm, run_row_hbm, run_col_hbm,
    k_ref, v_ref, decay_ref, sent_ref, run_row_ref, run_col_ref, k_sem, v_sem, out_sem, small_sem,
):
    load_decay = pltpu.make_async_copy(decay_hbm, decay_ref, small_sem.at[0])
    loads = pieces(k_hbm, k_ref, k_sem) + pieces(v_hbm, v_ref, v_sem)
    load_decay.start()
    start(loads)
    ones = jnp.where(causal(), 1.0, 0.0).astype(F32)
    load_decay.wait()
    decay = decay_ref[...]
    run_row = dot(decay, ones, NT, lax.Precision.HIGHEST)
    run_col = dot(ones, decay, NT, lax.Precision.HIGHEST)
    run_row_ref[...] = run_row
    run_col_ref[...] = run_col
    totals = jnp.broadcast_to(run_row[:, T - 1 : T], (HEADS, E))
    small = [
        pltpu.make_async_copy(run_row_ref, run_row_hbm, small_sem.at[1]),
        pltpu.make_async_copy(run_col_ref, run_col_hbm, small_sem.at[2]),
    ]
    start(small)
    shrink = jnp.exp(run_col[T - 1 : T, :] - run_col)
    wait(loads)
    for half in range(2):
        for h in range(half * HEADS // 2, (half + 1) * HEADS // 2):
            key_dec = (k_ref[:, lanes(h)].astype(F32) * shrink[:, h : h + 1]).astype(BF16)
            state = dot(key_dec, v_ref[:, lanes(h)], TN)
            for i in range(PER_HEAD):
                row = (h * PER_HEAD + i) * SPAN
                sent_ref[row : row + ROWS] = state[i * ROWS : (i + 1) * ROWS]
                sent_ref[row + ROWS : row + SPAN] = totals[h : h + 1]
        start(half_copies([(sent_ref, sent_hbm, out_sem)], half, False))
    wait(small)
    for half in range(2):
        wait(half_copies([(sent_ref, sent_hbm, out_sem)], half, False))


def local_kernel(
    q_hbm, k_hbm, v_hbm, run_row_ref, run_col_ref, weights_hbm, mixed_ref, query_dec_ref,
    q_ref, k_ref, v_ref, weights_ref, q_sem, k_sem, v_sem, out_sem,
):
    loads = pieces(q_hbm, q_ref, q_sem) + pieces(k_hbm, k_ref, k_sem) + pieces(v_hbm, v_ref, v_sem)
    start(loads)
    mask = causal()
    growth = jnp.exp(run_col_ref[...])
    wait(loads)
    for h in range(HEADS):
        q = q_ref[:, lanes(h)]
        gap = run_col_ref[:, h : h + 1] - run_row_ref[h : h + 1, :]
        decay = jnp.exp(jnp.where(mask, gap, -1e30))
        scores = dot(q, k_ref[:, lanes(h)], NT)
        weights = (scores * SCALING * decay).astype(BF16)
        weights_ref[h] = weights
        mixed_ref[:, lanes(h)] = dot(weights, v_ref[:, lanes(h)], NN)
        query_dec_ref[:, lanes(h)] = (q.astype(F32) * growth[:, h : h + 1]).astype(BF16)
    stores = pieces(weights_ref, weights_hbm, out_sem)
    start(stores)
    wait(stores)


def mixed_kernel(
    mixed_ref, query_dec_ref, g_ref, entering_ref, attended_hbm, grad_mixed_hbm, state_hbm, half_hbm,
    attended_ref, grad_mixed_ref, state_ref, half_ref, attended_sem, grad_mixed_sem, state_sem, half_sem,
):
    def send(half):
        tall = [(state_ref, state_hbm, state_sem), (half_ref, half_hbm, half_sem)]
        wide = [(attended_ref, attended_hbm, attended_sem), (grad_mixed_ref, grad_mixed_hbm, grad_mixed_sem)]
        return half_copies(tall, half, False) + half_copies(wide, half, True)

    for half in range(2):
        for h in range(half * HEADS // 2, (half + 1) * HEADS // 2):
            query_dec = query_dec_ref[:, lanes(h)]
            entering = entering_ref[h].astype(BF16)
            half_ref[h] = entering
            mixed = mixed_ref[:, lanes(h)] + SCALING * dot(query_dec, entering, NN)
            inverse = lax.rsqrt(jnp.mean(mixed * mixed, axis=1, keepdims=True) + EPSILON)
            normed = mixed * inverse
            attended_ref[:, lanes(h)] = normed.astype(BF16)
            g = g_ref[:, lanes(h)].astype(F32)
            grad_mixed = inverse * (g - normed * jnp.mean(g * normed, axis=1, keepdims=True))
            grad_mixed = grad_mixed.astype(BF16)
            grad_mixed_ref[:, lanes(h)] = grad_mixed
            state_ref[h] = SCALING * dot(query_dec, grad_mixed, TN)
        start(send(half))
    for half in range(2):
        wait(send(half))


def local_grads_kernel(
    q_hbm, k_hbm, v_hbm, weights_hbm, run_row_ref, run_col_ref, grad_mixed_ref, half_ref,
    grad_q_hbm, part_k_ref, part_v_ref,
    q_ref, k_ref, v_ref, weights_ref, grad_q_ref, q_sem, k_sem, v_sem, w_sem, out_sem,
):
    loads = pieces(q_hbm, q_ref, q_sem) + pieces(k_hbm, k_ref, k_sem)
    loads += pieces(v_hbm, v_ref, v_sem) + pieces(weights_hbm, weights_ref, w_sem)
    start(loads)
    mask = causal()
    growth = jnp.exp(run_col_ref[...]) * SCALING
    wait(loads)
    for h in range(HEADS):
        grad_mixed = grad_mixed_ref[:, lanes(h)]
        gap = run_col_ref[:, h : h + 1] - run_row_ref[h : h + 1, :]
        decay = jnp.exp(jnp.where(mask, gap, -1e30))
        grad_prob = dot(grad_mixed, v_ref[:, lanes(h)], NT)
        grad_score = (grad_prob * SCALING * decay).astype(BF16)
        grad_q = dot(grad_score, k_ref[:, lanes(h)], NN)
        grad_q = grad_q + growth[:, h : h + 1] * dot(grad_mixed, half_ref[h], NT)
        grad_q_ref[:, lanes(h)] = grad_q.astype(BF16)
        part_k_ref[:, lanes(h)] = dot(grad_score, q_ref[:, lanes(h)], TN)
        part_v_ref[:, lanes(h)] = dot(weights_ref[h], grad_mixed, TN)
    stores = pieces(grad_q_ref, grad_q_hbm, out_sem)
    start(stores)
    wait(stores)


def final_kernel(
    k_ref, v_ref, run_col_ref, part_k_ref, part_v_hbm, leaving_ref, grad_k_hbm, grad_v_hbm,
    part_v_ref, grad_k_ref, grad_v_ref, in_sem, k_sem, v_sem,
):
    loads = pieces(part_v_hbm, part_v_ref, in_sem)
    start(loads)
    run_col = run_col_ref[...]
    shrink = jnp.exp(run_col[T - 1 : T, :] - run_col)
    for h in range(HEADS):
        grad_k = shrink[:, h : h + 1] * dot(v_ref[:, lanes(h)], leaving_ref[h].astype(BF16), NT)
        grad_k_ref[:, lanes(h)] = (part_k_ref[:, lanes(h)] + grad_k).astype(BF16)
    store_k = pieces(grad_k_ref, grad_k_hbm, k_sem)
    start(store_k)
    wait(loads)
    for h in range(HEADS):
        key_dec = (k_ref[:, lanes(h)].astype(F32) * shrink[:, h : h + 1]).astype(BF16)
        grad_v = dot(key_dec, leaving_ref[h].astype(BF16), NN)
        grad_v_ref[:, lanes(h)] = (part_v_ref[:, lanes(h)] + grad_v).astype(BF16)
    store_v = pieces(grad_v_ref, grad_v_hbm, v_sem)
    start(store_v)
    wait(store_k + store_v)


def group_total_kernel(recv_ref, total_ref, decays_ref):
    total = recv_ref[:ROWS]
    logs = recv_ref[ROWS:SPAN]
    decays_ref[0:1, :] = jnp.exp(logs)
    for j in range(1, PEERS):
        log = recv_ref[j * SPAN + ROWS : (j + 1) * SPAN]
        decay = jnp.exp(log)
        decays_ref[j : j + 1, :] = decay
        total = decay * total + recv_ref[j * SPAN : j * SPAN + ROWS]
        logs = logs + log
    total_ref[:ROWS, :] = total
    total_ref[ROWS:, :] = jnp.broadcast_to(jnp.exp(logs), (8, E))


def back_total_kernel(recv_ref, decays_ref, total_ref):
    total = recv_ref[(PEERS - 1) * ROWS :]
    for j in reversed(range(PEERS - 1)):
        total = decays_ref[j : j + 1, :] * total + recv_ref[j * ROWS : (j + 1) * ROWS]
    total_ref[...] = total


def both_kernel(reverse, mine_ref, other_ref, decay_mine_ref, decay_other_ref, both_ref):
    mine, other = mine_ref[:ROWS, :], other_ref[:ROWS, :]
    decay_mine, decay_other = decay_mine_ref[ROWS : ROWS + 1, :], decay_other_ref[ROWS : ROWS + 1, :]
    core = lax.axis_index("core")
    mine_last = (core == 0) if reverse else (core == 1)
    both = jnp.where(mine_last, decay_mine * other + mine, decay_other * mine + other)
    both_ref[:ROWS, :] = both
    if not reverse:
        both_ref[ROWS:, :] = jnp.broadcast_to(decay_mine * decay_other, (8, E))


def spread_kernel(
    reverse, recv_ref, decays_ref, far3_ref, far2_ref, far1_ref, other_ref,
    decay3_ref, decay2_ref, decay1_ref, decay_other_ref, out_ref,
):
    y, core = lax.axis_index("y"), lax.axis_index("core")
    span = recv_ref.shape[0] // PEERS
    state = jnp.zeros((ROWS, E), F32)
    steps = [(far3_ref, decay3_ref, 3), (far2_ref, decay2_ref, 2), (far1_ref, decay1_ref, 1)]
    for far_ref, decay_ref, by in steps:
        counts = (y + by < 4) if reverse else (y >= by)
        stepped = decay_ref[ROWS : ROWS + 1, :] * state + far_ref[:ROWS, :]
        state = jnp.where(counts, stepped, state)
    counts = (core == 0) if reverse else (core == 1)
    state = jnp.where(counts, decay_other_ref[ROWS : ROWS + 1, :] * state + other_ref[:ROWS, :], state)
    for j in reversed(range(PEERS)) if reverse else range(PEERS):
        out_ref[j] = state
        state = decays_ref[j : j + 1, :] * state + recv_ref[j * span : j * span + ROWS]


def shifted(array, by):
    return lax.ppermute(array, "y", [(i, (i + by) % 4) for i in range(4)])


def swapped(array):
    return lax.ppermute(array, "core", [(0, 1), (1, 0)])


def exchanged(array):
    return lax.all_to_all(array, GROUP, 0, 0, tiled=True)


def both_of(reverse, rows, *args):
    return call(lambda *refs: both_kernel(reverse, *refs), [((rows, E), F32)], *args)[0]


def spread(reverse, *args):
    return call(lambda *refs: spread_kernel(reverse, *refs), [((PEERS, ROWS, E), F32)], *args)[0]


def body(q, k, v, log_decay, g):
    wide = (T, HEADS * E)
    narrow = pltpu.VMEM(wide, BF16)
    square = pltpu.VMEM((HEADS, T, T), BF16)
    sems, two = pltpu.SemaphoreType.DMA((PIECES,)), pltpu.SemaphoreType.DMA((2,))

    sent, run_row, run_col = call(
        states_kernel, [((PEERS * SPAN, E), F32), ((HEADS, T), F32), ((T, HEADS), F32)],
        k, v, log_decay, flops=2 * HEADS * T * E * E, hbm_in=(0, 1, 2), hbm_out=(0, 1, 2),
        scratch=[
            narrow, narrow, pltpu.VMEM((HEADS, T), F32), pltpu.VMEM((PEERS * SPAN, E), F32),
            pltpu.VMEM((HEADS, T), F32), pltpu.VMEM((T, HEADS), F32), sems, sems, two, sems,
        ],
    )
    recv = exchanged(sent.reshape(PEERS, 1, SPAN * E)).reshape(PEERS * SPAN, E)
    weights, mixed_part, query_dec = call(
        local_kernel, [((HEADS, T, T), BF16), (wide, F32), (wide, BF16)],
        q, k, v, run_row, run_col, flops=4 * HEADS * T * T * E, hbm_in=(0, 1, 2), hbm_out=(0,),
        scratch=[narrow, narrow, narrow, square, sems, sems, sems, sems],
    )
    recv, mixed_part, query_dec = lax.optimization_barrier((recv, mixed_part, query_dec))
    total, decays = call(
        group_total_kernel, [((ROWS + 8, E), F32), ((PEERS, E), F32)], recv,
    )
    other = swapped(total)
    both = both_of(False, ROWS + 8, total, other, total, other)
    far3, far2, far1 = [shifted(both, by) for by in (3, 2, 1)]
    entering = exchanged(spread(False, recv, decays, far3, far2, far1, other, far3, far2, far1, other))
    entering = entering.reshape(HEADS, E, E)

    attended, grad_mixed, state, half = call(
        mixed_kernel, [(wide, BF16), (wide, BF16), ((HEADS, E, E), F32), ((HEADS, E, E), BF16)],
        mixed_part, query_dec, g, entering, flops=4 * HEADS * T * E * E, hbm_out=(0, 1, 2, 3),
        scratch=[narrow, narrow, pltpu.VMEM((HEADS, E, E), F32), pltpu.VMEM((HEADS, E, E), BF16), two, two, two, two],
    )
    recv = exchanged(state.reshape(PEERS, ROWS, E)).reshape(PEERS * ROWS, E)
    grad_q, part_k, part_v = call(
        local_grads_kernel, [(wide, BF16), (wide, F32), (wide, F32)],
        q, k, v, weights, run_row, run_col, grad_mixed, half, flops=9 * HEADS * T * T * E,
        hbm_in=(0, 1, 2, 3), hbm_out=(0,),
        scratch=[narrow, narrow, narrow, square, narrow, sems, sems, sems, sems, sems],
    )
    recv, part_k, part_v = lax.optimization_barrier((recv, part_k, part_v))
    back_total = call(back_total_kernel, [((ROWS, E), F32)], recv, decays)[0]
    back_other = swapped(back_total)
    back_both = both_of(True, ROWS, back_total, back_other, total, other)
    back3, back2, back1 = [shifted(back_both, -by) for by in (3, 2, 1)]
    leaving = exchanged(spread(True, recv, decays, back3, back2, back1, back_other, far1, far2, far3, other))
    leaving = leaving.reshape(HEADS, E, E)
    grad_k, grad_v = call(
        final_kernel, [(wide, BF16), (wide, BF16)],
        k, v, run_col, part_k, part_v, leaving, flops=4 * HEADS * T * E * E, hbm_in=(4,), hbm_out=(0, 1),
        scratch=[pltpu.VMEM(wide, F32), narrow, narrow, sems, sems, sems],
    )
    return attended, grad_q, grad_k, grad_v


def solution(mesh):
    finer = Mesh(mesh.devices.reshape(4, 2, 4, 8), ALL)
    rows = P(ALL, None)
    return jax.shard_map(
        body,
        mesh=finer,
        in_specs=(rows, rows, rows, P(None, ALL), rows),
        out_specs=(rows, rows, rows, rows),
        check_vma=False,
    )
```

```python
import math

import jax
import jax.numpy as jnp
from jax import lax
from jax.experimental import pallas as pl
from jax.experimental.pallas import tpu as pltpu
from jax.sharding import Mesh
from jax.sharding import PartitionSpec as P

ALL = ("y", "core", "x", "z")
GROUP = ("x", "z")
EPSILON = 1e-06
HEADS = 8
E = 128
T = 256
PEERS = 32
ROWS = HEADS * E // PEERS
PER_HEAD = PEERS // HEADS
SPAN = ROWS + 1
PIECES = 1
SCALING = 1.0 / math.sqrt(E)
F32 = jnp.float32
BF16 = jnp.bfloat16


def dot(a, b, dims, precision=None):
    return lax.dot_general(a, b, (dims, ((), ())), precision=precision, preferred_element_type=F32)


NN, NT, TN = ((1,), (0,)), ((1,), (1,)), ((0,), (0,))


def lanes(h):
    return slice(h * E, (h + 1) * E)


def causal():
    t = lax.broadcasted_iota(jnp.int32, (T, T), 0)
    s = lax.broadcasted_iota(jnp.int32, (T, T), 1)
    return s <= t


def call(kernel, outs, *args, smem=0, flops=0, hbm_in=(), hbm_out=(), scratch=(), grant=16):
    def spec(space):
        return pl.BlockSpec(memory_space=space)

    ins = [spec(pltpu.SMEM if i < smem else pltpu.HBM if i in hbm_in else pltpu.VMEM) for i in range(len(args))]
    moved = sum(a.size * a.dtype.itemsize for a in args)
    moved += sum(math.prod(s) * jnp.dtype(d).itemsize for s, d in outs)
    return pl.pallas_call(
        kernel,
        out_shape=[pltpu.HBM(s, d) if i in hbm_out else jax.ShapeDtypeStruct(s, d) for i, (s, d) in enumerate(outs)],
        in_specs=ins,
        out_specs=[spec(pltpu.HBM if i in hbm_out else pltpu.VMEM) for i in range(len(outs))],
        scratch_shapes=scratch,
        cost_estimate=pl.CostEstimate(flops=flops, bytes_accessed=moved, transcendentals=0),
        compiler_params=pltpu.CompilerParams(vmem_limit_bytes=grant * 1024 * 1024),
    )(*[pltpu.with_memory_space_constraint(a, pltpu.HBM) if i in hbm_in else a for i, a in enumerate(args)])


def pieces(source, target, sems, count=PIECES):
    size = source.shape[0] // count
    return [
        pltpu.make_async_copy(source.at[pl.ds(i * size, size)], target.at[pl.ds(i * size, size)], sems.at[i])
        for i in range(count)
    ]


def start(copies):
    for copy in copies:
        copy.start()


def wait(copies):
    for copy in copies:
        copy.wait()


def half_copies(pairs, half, wide):
    copies = []
    for source, target, sem in pairs:
        if wide:
            here = pl.ds(half * HEADS * E // 2, HEADS * E // 2)
            copies.append(pltpu.make_async_copy(source.at[:, here], target.at[:, here], sem.at[half]))
        else:
            size = source.shape[0] // 2
            here = pl.ds(half * size, size)
            copies.append(pltpu.make_async_copy(source.at[here], target.at[here], sem.at[half]))
    return copies


def states_kernel(
    k_hbm, v_hbm, decay_hbm, sent_hbm, run_row_hbm, run_col_hbm,
    k_ref, v_ref, decay_ref, sent_ref, run_row_ref, run_col_ref, k_sem, v_sem, out_sem, small_sem,
):
    load_decay = pltpu.make_async_copy(decay_hbm, decay_ref, small_sem.at[0])
    loads = pieces(k_hbm, k_ref, k_sem) + pieces(v_hbm, v_ref, v_sem)
    load_decay.start()
    start(loads)
    ones = jnp.where(causal(), 1.0, 0.0).astype(F32)
    load_decay.wait()
    decay = decay_ref[...]
    run_row = dot(decay, ones, NT, lax.Precision.HIGHEST)
    run_col = dot(ones, decay, NT, lax.Precision.HIGHEST)
    run_row_ref[...] = run_row
    run_col_ref[...] = run_col
    totals = jnp.broadcast_to(run_row[:, T - 1 : T], (HEADS, E))
    small = [
        pltpu.make_async_copy(run_row_ref, run_row_hbm, small_sem.at[1]),
        pltpu.make_async_copy(run_col_ref, run_col_hbm, small_sem.at[2]),
    ]
    start(small)
    shrink = jnp.exp(run_col[T - 1 : T, :] - run_col)
    wait(loads)
    for half in range(2):
        for h in range(half * HEADS // 2, (half + 1) * HEADS // 2):
            key_dec = (k_ref[:, lanes(h)].astype(F32) * shrink[:, h : h + 1]).astype(BF16)
            state = dot(key_dec, v_ref[:, lanes(h)], TN)
            for i in range(PER_HEAD):
                row = (h * PER_HEAD + i) * SPAN
                sent_ref[row : row + ROWS] = state[i * ROWS : (i + 1) * ROWS]
                sent_ref[row + ROWS : row + SPAN] = totals[h : h + 1]
        start(half_copies([(sent_ref, sent_hbm, out_sem)], half, False))
    wait(small)
    for half in range(2):
        wait(half_copies([(sent_ref, sent_hbm, out_sem)], half, False))


def local_kernel(
    q_hbm, k_hbm, v_hbm, run_row_ref, run_col_ref, weights_hbm, mixed_ref, query_dec_ref,
    q_ref, k_ref, v_ref, weights_ref, q_sem, k_sem, v_sem, out_sem,
):
    loads = pieces(q_hbm, q_ref, q_sem) + pieces(k_hbm, k_ref, k_sem) + pieces(v_hbm, v_ref, v_sem)
    start(loads)
    mask = causal()
    growth = jnp.exp(run_col_ref[...])
    wait(loads)
    for h in range(HEADS):
        q = q_ref[:, lanes(h)]
        gap = run_col_ref[:, h : h + 1] - run_row_ref[h : h + 1, :]
        decay = jnp.exp(jnp.where(mask, gap, -1e30))
        scores = dot(q, k_ref[:, lanes(h)], NT)
        weights = (scores * SCALING * decay).astype(BF16)
        weights_ref[h] = weights
        mixed_ref[:, lanes(h)] = dot(weights, v_ref[:, lanes(h)], NN)
        query_dec_ref[:, lanes(h)] = (q.astype(F32) * growth[:, h : h + 1]).astype(BF16)
    stores = pieces(weights_ref, weights_hbm, out_sem)
    start(stores)
    wait(stores)


def mixed_kernel(
    mixed_ref, query_dec_ref, g_ref, entering_ref, attended_hbm, grad_mixed_hbm, state_hbm, half_hbm,
    attended_ref, grad_mixed_ref, state_ref, half_ref, attended_sem, grad_mixed_sem, state_sem, half_sem,
):
    def send(half):
        tall = [(state_ref, state_hbm, state_sem), (half_ref, half_hbm, half_sem)]
        wide = [(attended_ref, attended_hbm, attended_sem), (grad_mixed_ref, grad_mixed_hbm, grad_mixed_sem)]
        return half_copies(tall, half, False) + half_copies(wide, half, True)

    for half in range(2):
        for h in range(half * HEADS // 2, (half + 1) * HEADS // 2):
            query_dec = query_dec_ref[:, lanes(h)]
            entering = entering_ref[h].astype(BF16)
            half_ref[h] = entering
            mixed = mixed_ref[:, lanes(h)] + SCALING * dot(query_dec, entering, NN)
            inverse = lax.rsqrt(jnp.mean(mixed * mixed, axis=1, keepdims=True) + EPSILON)
            normed = mixed * inverse
            attended_ref[:, lanes(h)] = normed.astype(BF16)
            g = g_ref[:, lanes(h)].astype(F32)
            grad_mixed = inverse * (g - normed * jnp.mean(g * normed, axis=1, keepdims=True))
            grad_mixed = grad_mixed.astype(BF16)
            grad_mixed_ref[:, lanes(h)] = grad_mixed
            state_ref[h] = SCALING * dot(query_dec, grad_mixed, TN)
        start(send(half))
    for half in range(2):
        wait(send(half))


def local_grads_kernel(
    q_hbm, k_hbm, v_hbm, weights_hbm, run_row_ref, run_col_ref, grad_mixed_ref, half_ref,
    grad_q_hbm, part_k_ref, part_v_ref,
    q_ref, k_ref, v_ref, weights_ref, grad_q_ref, q_sem, k_sem, v_sem, w_sem, out_sem,
):
    loads = pieces(q_hbm, q_ref, q_sem) + pieces(k_hbm, k_ref, k_sem)
    loads += pieces(v_hbm, v_ref, v_sem) + pieces(weights_hbm, weights_ref, w_sem)
    start(loads)
    mask = causal()
    growth = jnp.exp(run_col_ref[...]) * SCALING
    wait(loads)
    for h in range(HEADS):
        grad_mixed = grad_mixed_ref[:, lanes(h)]
        gap = run_col_ref[:, h : h + 1] - run_row_ref[h : h + 1, :]
        decay = jnp.exp(jnp.where(mask, gap, -1e30))
        grad_prob = dot(grad_mixed, v_ref[:, lanes(h)], NT)
        grad_score = (grad_prob * SCALING * decay).astype(BF16)
        grad_q = dot(grad_score, k_ref[:, lanes(h)], NN)
        grad_q = grad_q + growth[:, h : h + 1] * dot(grad_mixed, half_ref[h], NT)
        grad_q_ref[:, lanes(h)] = grad_q.astype(BF16)
        part_k_ref[:, lanes(h)] = dot(grad_score, q_ref[:, lanes(h)], TN)
        part_v_ref[:, lanes(h)] = dot(weights_ref[h], grad_mixed, TN)
    stores = pieces(grad_q_ref, grad_q_hbm, out_sem)
    start(stores)
    wait(stores)


def final_kernel(
    k_ref, v_ref, run_col_ref, part_k_ref, part_v_hbm, leaving_ref, grad_k_hbm, grad_v_hbm,
    part_v_ref, grad_k_ref, grad_v_ref, in_sem, k_sem, v_sem,
):
    loads = pieces(part_v_hbm, part_v_ref, in_sem)
    start(loads)
    run_col = run_col_ref[...]
    shrink = jnp.exp(run_col[T - 1 : T, :] - run_col)
    for h in range(HEADS):
        grad_k = shrink[:, h : h + 1] * dot(v_ref[:, lanes(h)], leaving_ref[h].astype(BF16), NT)
        grad_k_ref[:, lanes(h)] = (part_k_ref[:, lanes(h)] + grad_k).astype(BF16)
    store_k = pieces(grad_k_ref, grad_k_hbm, k_sem)
    start(store_k)
    wait(loads)
    for h in range(HEADS):
        key_dec = (k_ref[:, lanes(h)].astype(F32) * shrink[:, h : h + 1]).astype(BF16)
        grad_v = dot(key_dec, leaving_ref[h].astype(BF16), NN)
        grad_v_ref[:, lanes(h)] = (part_v_ref[:, lanes(h)] + grad_v).astype(BF16)
    store_v = pieces(grad_v_ref, grad_v_hbm, v_sem)
    start(store_v)
    wait(store_k + store_v)


def group_total_kernel(recv_ref, total_ref, decays_ref):
    total = recv_ref[:ROWS]
    logs = recv_ref[ROWS:SPAN]
    decays_ref[0:1, :] = jnp.exp(logs)
    for j in range(1, PEERS):
        log = recv_ref[j * SPAN + ROWS : (j + 1) * SPAN]
        decay = jnp.exp(log)
        decays_ref[j : j + 1, :] = decay
        total = decay * total + recv_ref[j * SPAN : j * SPAN + ROWS]
        logs = logs + log
    total_ref[:ROWS, :] = total
    total_ref[ROWS:, :] = jnp.broadcast_to(jnp.exp(logs), (8, E))


def back_total_kernel(recv_ref, decays_ref, total_ref):
    total = recv_ref[(PEERS - 1) * ROWS :]
    for j in reversed(range(PEERS - 1)):
        total = decays_ref[j : j + 1, :] * total + recv_ref[j * ROWS : (j + 1) * ROWS]
    total_ref[...] = total


def both_kernel(reverse, mine_ref, other_ref, decay_mine_ref, decay_other_ref, both_ref):
    mine, other = mine_ref[:ROWS, :], other_ref[:ROWS, :]
    decay_mine, decay_other = decay_mine_ref[ROWS : ROWS + 1, :], decay_other_ref[ROWS : ROWS + 1, :]
    core = lax.axis_index("core")
    mine_last = (core == 0) if reverse else (core == 1)
    both = jnp.where(mine_last, decay_mine * other + mine, decay_other * mine + other)
    both_ref[:ROWS, :] = both
    if not reverse:
        both_ref[ROWS:, :] = jnp.broadcast_to(decay_mine * decay_other, (8, E))


def spread_kernel(
    reverse, recv_ref, decays_ref, far3_ref, far2_ref, far1_ref, other_ref,
    decay3_ref, decay2_ref, decay1_ref, decay_other_ref, out_ref,
):
    y, core = lax.axis_index("y"), lax.axis_index("core")
    span = recv_ref.shape[0] // PEERS
    state = jnp.zeros((ROWS, E), F32)
    steps = [(far3_ref, decay3_ref, 3), (far2_ref, decay2_ref, 2), (far1_ref, decay1_ref, 1)]
    for far_ref, decay_ref, by in steps:
        counts = (y + by < 4) if reverse else (y >= by)
        stepped = decay_ref[ROWS : ROWS + 1, :] * state + far_ref[:ROWS, :]
        state = jnp.where(counts, stepped, state)
    counts = (core == 0) if reverse else (core == 1)
    state = jnp.where(counts, decay_other_ref[ROWS : ROWS + 1, :] * state + other_ref[:ROWS, :], state)
    for j in reversed(range(PEERS)) if reverse else range(PEERS):
        out_ref[j] = state
        state = decays_ref[j : j + 1, :] * state + recv_ref[j * span : j * span + ROWS]


def shifted(array, by):
    return lax.ppermute(array, "y", [(i, (i + by) % 4) for i in range(4)])


def swapped(array):
    return lax.ppermute(array, "core", [(0, 1), (1, 0)])


def exchanged(array):
    return lax.all_to_all(array, GROUP, 0, 0, tiled=True)


def both_of(reverse, rows, *args):
    return call(lambda *refs: both_kernel(reverse, *refs), [((rows, E), F32)], *args)[0]


def spread(reverse, *args):
    return call(lambda *refs: spread_kernel(reverse, *refs), [((PEERS, ROWS, E), F32)], *args)[0]


def body(q, k, v, log_decay, g):
    wide = (T, HEADS * E)
    narrow = pltpu.VMEM(wide, BF16)
    square = pltpu.VMEM((HEADS, T, T), BF16)
    sems, two = pltpu.SemaphoreType.DMA((PIECES,)), pltpu.SemaphoreType.DMA((2,))

    sent, run_row, run_col = call(
        states_kernel, [((PEERS * SPAN, E), F32), ((HEADS, T), F32), ((T, HEADS), F32)],
        k, v, log_decay, flops=2 * HEADS * T * E * E, hbm_in=(0, 1, 2), hbm_out=(0, 1, 2),
        scratch=[
            narrow, narrow, pltpu.VMEM((HEADS, T), F32), pltpu.VMEM((PEERS * SPAN, E), F32),
            pltpu.VMEM((HEADS, T), F32), pltpu.VMEM((T, HEADS), F32), sems, sems, two, pltpu.SemaphoreType.DMA((3,)),
        ],
    )
    recv = exchanged(sent.reshape(PEERS, 1, SPAN * E)).reshape(PEERS * SPAN, E)
    weights, mixed_part, query_dec = call(
        local_kernel, [((HEADS, T, T), BF16), (wide, F32), (wide, BF16)],
        q, k, v, run_row, run_col, flops=4 * HEADS * T * T * E, hbm_in=(0, 1, 2), hbm_out=(0,),
        scratch=[narrow, narrow, narrow, square, sems, sems, sems, sems],
    )
    recv, mixed_part, query_dec = lax.optimization_barrier((recv, mixed_part, query_dec))
    total, decays = call(
        group_total_kernel, [((ROWS + 8, E), F32), ((PEERS, E), F32)], recv,
    )
    other = swapped(total)
    both = both_of(False, ROWS + 8, total, other, total, other)
    far3, far2, far1 = [shifted(both, by) for by in (3, 2, 1)]
    entering = exchanged(spread(False, recv, decays, far3, far2, far1, other, far3, far2, far1, other))
    entering = entering.reshape(HEADS, E, E)

    attended, grad_mixed, state, half = call(
        mixed_kernel, [(wide, BF16), (wide, BF16), ((HEADS, E, E), F32), ((HEADS, E, E), BF16)],
        mixed_part, query_dec, g, entering, flops=4 * HEADS * T * E * E, hbm_out=(0, 1, 2, 3),
        scratch=[narrow, narrow, pltpu.VMEM((HEADS, E, E), F32), pltpu.VMEM((HEADS, E, E), BF16), two, two, two, two],
    )
    recv = exchanged(state.reshape(PEERS, ROWS, E)).reshape(PEERS * ROWS, E)
    grad_q, part_k, part_v = call(
        local_grads_kernel, [(wide, BF16), (wide, F32), (wide, F32)],
        q, k, v, weights, run_row, run_col, grad_mixed, half, flops=9 * HEADS * T * T * E,
        hbm_in=(0, 1, 2, 3), hbm_out=(0,),
        scratch=[narrow, narrow, narrow, square, narrow, sems, sems, sems, sems, sems],
    )
    recv, part_k, part_v = lax.optimization_barrier((recv, part_k, part_v))
    back_total = call(back_total_kernel, [((ROWS, E), F32)], recv, decays)[0]
    back_other = swapped(back_total)
    back_both = both_of(True, ROWS, back_total, back_other, total, other)
    back3, back2, back1 = [shifted(back_both, -by) for by in (3, 2, 1)]
    leaving = exchanged(spread(True, recv, decays, back3, back2, back1, back_other, far1, far2, far3, other))
    leaving = leaving.reshape(HEADS, E, E)
    grad_k, grad_v = call(
        final_kernel, [(wide, BF16), (wide, BF16)],
        k, v, run_col, part_k, part_v, leaving, flops=4 * HEADS * T * E * E, hbm_in=(4,), hbm_out=(0, 1),
        scratch=[pltpu.VMEM(wide, F32), narrow, narrow, sems, sems, sems],
    )
    return attended, grad_q, grad_k, grad_v


def solution(mesh):
    finer = Mesh(mesh.devices.reshape(4, 2, 4, 8), ALL)
    rows = P(ALL, None)
    return jax.shard_map(
        body,
        mesh=finer,
        in_specs=(rows, rows, rows, P(None, ALL), rows),
        out_specs=(rows, rows, rows, rows),
        check_vma=False,
    )
```

```python
import math

import jax
import jax.numpy as jnp
from jax import lax
from jax.experimental import pallas as pl
from jax.experimental.pallas import tpu as pltpu
from jax.sharding import Mesh
from jax.sharding import PartitionSpec as P

ALL = ("y", "core", "x", "z")
GROUP = ("x", "z")
EPSILON = 1e-06
HEADS = 8
E = 128
T = 256
PEERS = 32
ROWS = HEADS * E // PEERS
PER_HEAD = PEERS // HEADS
SPAN = ROWS + 1
PIECES = 1
SCALING = 1.0 / math.sqrt(E)
F32 = jnp.float32
BF16 = jnp.bfloat16


def dot(a, b, dims, precision=None):
    return lax.dot_general(a, b, (dims, ((), ())), precision=precision, preferred_element_type=F32)


NN, NT, TN = ((1,), (0,)), ((1,), (1,)), ((0,), (0,))


def lanes(h):
    return slice(h * E, (h + 1) * E)


def causal():
    t = lax.broadcasted_iota(jnp.int32, (T, T), 0)
    s = lax.broadcasted_iota(jnp.int32, (T, T), 1)
    return s <= t


def call(kernel, outs, *args, smem=0, flops=0, hbm_in=(), hbm_out=(), scratch=(), grant=16):
    def spec(space):
        return pl.BlockSpec(memory_space=space)

    ins = [spec(pltpu.SMEM if i < smem else pltpu.HBM if i in hbm_in else pltpu.VMEM) for i in range(len(args))]
    moved = sum(a.size * a.dtype.itemsize for a in args)
    moved += sum(math.prod(s) * jnp.dtype(d).itemsize for s, d in outs)
    return pl.pallas_call(
        kernel,
        out_shape=[pltpu.HBM(s, d) if i in hbm_out else jax.ShapeDtypeStruct(s, d) for i, (s, d) in enumerate(outs)],
        in_specs=ins,
        out_specs=[spec(pltpu.HBM if i in hbm_out else pltpu.VMEM) for i in range(len(outs))],
        scratch_shapes=scratch,
        cost_estimate=pl.CostEstimate(flops=flops, bytes_accessed=moved, transcendentals=0),
        compiler_params=pltpu.CompilerParams(vmem_limit_bytes=grant * 1024 * 1024),
    )(*[pltpu.with_memory_space_constraint(a, pltpu.HBM) if i in hbm_in else a for i, a in enumerate(args)])


def pieces(source, target, sems, count=PIECES):
    size = source.shape[0] // count
    return [
        pltpu.make_async_copy(source.at[pl.ds(i * size, size)], target.at[pl.ds(i * size, size)], sems.at[i])
        for i in range(count)
    ]


def start(copies):
    for copy in copies:
        copy.start()


def wait(copies):
    for copy in copies:
        copy.wait()


def half_copies(pairs, half, wide):
    copies = []
    for source, target, sem in pairs:
        if wide:
            here = pl.ds(half * HEADS * E // 2, HEADS * E // 2)
            copies.append(pltpu.make_async_copy(source.at[:, here], target.at[:, here], sem.at[half]))
        else:
            size = source.shape[0] // 2
            here = pl.ds(half * size, size)
            copies.append(pltpu.make_async_copy(source.at[here], target.at[here], sem.at[half]))
    return copies


def states_kernel(
    k_hbm, v_hbm, decay_hbm, sent_hbm, run_row_hbm, run_col_hbm,
    k_ref, v_ref, decay_ref, sent_ref, run_row_ref, run_col_ref, k_sem, v_sem, out_sem, small_sem,
):
    load_decay = pltpu.make_async_copy(decay_hbm, decay_ref, small_sem.at[0])
    loads = pieces(k_hbm, k_ref, k_sem) + pieces(v_hbm, v_ref, v_sem)
    load_decay.start()
    start(loads)
    ones = jnp.where(causal(), 1.0, 0.0).astype(F32)
    load_decay.wait()
    decay = decay_ref[...]
    run_row = dot(decay, ones, NT, lax.Precision.HIGHEST)
    run_col = dot(ones, decay, NT, lax.Precision.HIGHEST)
    run_row_ref[...] = run_row
    run_col_ref[...] = run_col
    totals = jnp.broadcast_to(run_row[:, T - 1 : T], (HEADS, E))
    small = [
        pltpu.make_async_copy(run_row_ref, run_row_hbm, small_sem.at[1]),
        pltpu.make_async_copy(run_col_ref, run_col_hbm, small_sem.at[2]),
    ]
    start(small)
    shrink = jnp.exp(run_col[T - 1 : T, :] - run_col)
    wait(loads)
    for half in range(2):
        for h in range(half * HEADS // 2, (half + 1) * HEADS // 2):
            key_dec = (k_ref[:, lanes(h)].astype(F32) * shrink[:, h : h + 1]).astype(BF16)
            state = dot(key_dec, v_ref[:, lanes(h)], TN)
            for i in range(PER_HEAD):
                row = (h * PER_HEAD + i) * SPAN
                sent_ref[row : row + ROWS] = state[i * ROWS : (i + 1) * ROWS]
                sent_ref[row + ROWS : row + SPAN] = totals[h : h + 1]
        start(half_copies([(sent_ref, sent_hbm, out_sem)], half, False))
    wait(small)
    for half in range(2):
        wait(half_copies([(sent_ref, sent_hbm, out_sem)], half, False))


def local_kernel(
    q_hbm, k_hbm, v_hbm, run_row_ref, run_col_ref, weights_hbm, mixed_ref, query_dec_ref,
    q_ref, k_ref, v_ref, weights_ref, q_sem, k_sem, v_sem, out_sem,
):
    loads = pieces(q_hbm, q_ref, q_sem) + pieces(k_hbm, k_ref, k_sem) + pieces(v_hbm, v_ref, v_sem)
    start(loads)
    mask = causal()
    growth = jnp.exp(run_col_ref[...])
    wait(loads)
    for h in range(HEADS):
        q = q_ref[:, lanes(h)]
        gap = run_col_ref[:, h : h + 1] - run_row_ref[h : h + 1, :]
        decay = jnp.exp(jnp.where(mask, gap, -1e30))
        scores = dot(q, k_ref[:, lanes(h)], NT)
        weights = (scores * SCALING * decay).astype(BF16)
        weights_ref[h] = weights
        mixed_ref[:, lanes(h)] = dot(weights, v_ref[:, lanes(h)], NN)
        query_dec_ref[:, lanes(h)] = (q.astype(F32) * growth[:, h : h + 1]).astype(BF16)
    stores = pieces(weights_ref, weights_hbm, out_sem)
    start(stores)
    wait(stores)


def mixed_kernel(
    mixed_ref, query_dec_ref, g_ref, entering_ref, attended_ref, grad_mixed_ref, state_hbm, half_hbm,
    state_ref, half_ref, state_sem, half_sem,
):
    def send(half):
        return half_copies([(state_ref, state_hbm, state_sem), (half_ref, half_hbm, half_sem)], half, False)

    for half in range(2):
        for h in range(half * HEADS // 2, (half + 1) * HEADS // 2):
            query_dec = query_dec_ref[:, lanes(h)]
            entering = entering_ref[h].astype(BF16)
            half_ref[h] = entering
            mixed = mixed_ref[:, lanes(h)] + SCALING * dot(query_dec, entering, NN)
            inverse = lax.rsqrt(jnp.mean(mixed * mixed, axis=1, keepdims=True) + EPSILON)
            normed = mixed * inverse
            attended_ref[:, lanes(h)] = normed.astype(BF16)
            g = g_ref[:, lanes(h)].astype(F32)
            grad_mixed = inverse * (g - normed * jnp.mean(g * normed, axis=1, keepdims=True))
            grad_mixed = grad_mixed.astype(BF16)
            grad_mixed_ref[:, lanes(h)] = grad_mixed
            state_ref[h] = SCALING * dot(query_dec, grad_mixed, TN)
        start(send(half))
    for half in range(2):
        wait(send(half))


def local_grads_kernel(
    q_hbm, k_hbm, v_hbm, weights_hbm, run_row_ref, run_col_ref, grad_mixed_ref, half_ref, attended_ref,
    grad_q_hbm, part_k_ref, part_v_ref, attended_hbm,
    q_ref, k_ref, v_ref, weights_ref, grad_q_ref, q_sem, k_sem, v_sem, w_sem, out_sem, attended_sem,
):
    store_attended = pieces(attended_ref, attended_hbm, attended_sem)
    start(store_attended)
    loads = pieces(q_hbm, q_ref, q_sem) + pieces(k_hbm, k_ref, k_sem)
    loads += pieces(v_hbm, v_ref, v_sem) + pieces(weights_hbm, weights_ref, w_sem)
    start(loads)
    mask = causal()
    growth = jnp.exp(run_col_ref[...]) * SCALING
    wait(loads)
    for h in range(HEADS):
        grad_mixed = grad_mixed_ref[:, lanes(h)]
        gap = run_col_ref[:, h : h + 1] - run_row_ref[h : h + 1, :]
        decay = jnp.exp(jnp.where(mask, gap, -1e30))
        grad_prob = dot(grad_mixed, v_ref[:, lanes(h)], NT)
        grad_score = (grad_prob * SCALING * decay).astype(BF16)
        grad_q = dot(grad_score, k_ref[:, lanes(h)], NN)
        grad_q = grad_q + growth[:, h : h + 1] * dot(grad_mixed, half_ref[h], NT)
        grad_q_ref[:, lanes(h)] = grad_q.astype(BF16)
        part_k_ref[:, lanes(h)] = dot(grad_score, q_ref[:, lanes(h)], TN)
        part_v_ref[:, lanes(h)] = dot(weights_ref[h], grad_mixed, TN)
    stores = pieces(grad_q_ref, grad_q_hbm, out_sem)
    start(stores)
    wait(stores + store_attended)


def final_kernel(
    k_ref, v_ref, run_col_ref, part_k_ref, part_v_hbm, leaving_ref, grad_k_hbm, grad_v_hbm,
    part_v_ref, grad_k_ref, grad_v_ref, in_sem, k_sem, v_sem,
):
    loads = [half_copies([(part_v_hbm, part_v_ref, in_sem)], half, True) for half in range(2)]
    start(loads[0] + loads[1])
    run_col = run_col_ref[...]
    shrink = jnp.exp(run_col[T - 1 : T, :] - run_col)
    for h in range(HEADS):
        grad_k = shrink[:, h : h + 1] * dot(v_ref[:, lanes(h)], leaving_ref[h].astype(BF16), NT)
        grad_k_ref[:, lanes(h)] = (part_k_ref[:, lanes(h)] + grad_k).astype(BF16)
    stores = pieces(grad_k_ref, grad_k_hbm, k_sem)
    start(stores)
    for half in range(2):
        wait(loads[half])
        for h in range(half * HEADS // 2, (half + 1) * HEADS // 2):
            key_dec = (k_ref[:, lanes(h)].astype(F32) * shrink[:, h : h + 1]).astype(BF16)
            grad_v = dot(key_dec, leaving_ref[h].astype(BF16), NN)
            grad_v_ref[:, lanes(h)] = (part_v_ref[:, lanes(h)] + grad_v).astype(BF16)
        store = half_copies([(grad_v_ref, grad_v_hbm, v_sem)], half, True)
        start(store)
        stores += store
    wait(stores)


def group_total_kernel(recv_ref, total_ref, decays_ref):
    total = recv_ref[:ROWS]
    logs = recv_ref[ROWS:SPAN]
    decays_ref[0:1, :] = jnp.exp(logs)
    for j in range(1, PEERS):
        log = recv_ref[j * SPAN + ROWS : (j + 1) * SPAN]
        decay = jnp.exp(log)
        decays_ref[j : j + 1, :] = decay
        total = decay * total + recv_ref[j * SPAN : j * SPAN + ROWS]
        logs = logs + log
    total_ref[:ROWS, :] = total
    total_ref[ROWS:, :] = jnp.broadcast_to(jnp.exp(logs), (8, E))


def back_total_kernel(recv_ref, decays_ref, total_ref):
    total = recv_ref[(PEERS - 1) * ROWS :]
    for j in reversed(range(PEERS - 1)):
        total = decays_ref[j : j + 1, :] * total + recv_ref[j * ROWS : (j + 1) * ROWS]
    total_ref[...] = total


def both_kernel(reverse, mine_ref, other_ref, decay_mine_ref, decay_other_ref, both_ref):
    mine, other = mine_ref[:ROWS, :], other_ref[:ROWS, :]
    decay_mine, decay_other = decay_mine_ref[ROWS : ROWS + 1, :], decay_other_ref[ROWS : ROWS + 1, :]
    core = lax.axis_index("core")
    mine_last = (core == 0) if reverse else (core == 1)
    both = jnp.where(mine_last, decay_mine * other + mine, decay_other * mine + other)
    both_ref[:ROWS, :] = both
    if not reverse:
        both_ref[ROWS:, :] = jnp.broadcast_to(decay_mine * decay_other, (8, E))


def spread_kernel(
    reverse, recv_ref, decays_ref, far3_ref, far2_ref, far1_ref, other_ref,
    decay3_ref, decay2_ref, decay1_ref, decay_other_ref, out_ref,
):
    y, core = lax.axis_index("y"), lax.axis_index("core")
    span = recv_ref.shape[0] // PEERS
    state = jnp.zeros((ROWS, E), F32)
    steps = [(far3_ref, decay3_ref, 3), (far2_ref, decay2_ref, 2), (far1_ref, decay1_ref, 1)]
    for far_ref, decay_ref, by in steps:
        counts = (y + by < 4) if reverse else (y >= by)
        stepped = decay_ref[ROWS : ROWS + 1, :] * state + far_ref[:ROWS, :]
        state = jnp.where(counts, stepped, state)
    counts = (core == 0) if reverse else (core == 1)
    state = jnp.where(counts, decay_other_ref[ROWS : ROWS + 1, :] * state + other_ref[:ROWS, :], state)
    for j in reversed(range(PEERS)) if reverse else range(PEERS):
        out_ref[j] = state
        state = decays_ref[j : j + 1, :] * state + recv_ref[j * span : j * span + ROWS]


def shifted(array, by):
    return lax.ppermute(array, "y", [(i, (i + by) % 4) for i in range(4)])


def swapped(array):
    return lax.ppermute(array, "core", [(0, 1), (1, 0)])


def exchanged(array):
    return lax.all_to_all(array, GROUP, 0, 0, tiled=True)


def both_of(reverse, rows, *args):
    return call(lambda *refs: both_kernel(reverse, *refs), [((rows, E), F32)], *args)[0]


def spread(reverse, *args):
    return call(lambda *refs: spread_kernel(reverse, *refs), [((PEERS, ROWS, E), F32)], *args)[0]


def body(q, k, v, log_decay, g):
    wide = (T, HEADS * E)
    narrow = pltpu.VMEM(wide, BF16)
    square = pltpu.VMEM((HEADS, T, T), BF16)
    sems, two = pltpu.SemaphoreType.DMA((PIECES,)), pltpu.SemaphoreType.DMA((2,))

    sent, run_row, run_col = call(
        states_kernel, [((PEERS * SPAN, E), F32), ((HEADS, T), F32), ((T, HEADS), F32)],
        k, v, log_decay, flops=2 * HEADS * T * E * E, hbm_in=(0, 1, 2), hbm_out=(0, 1, 2),
        scratch=[
            narrow, narrow, pltpu.VMEM((HEADS, T), F32), pltpu.VMEM((PEERS * SPAN, E), F32),
            pltpu.VMEM((HEADS, T), F32), pltpu.VMEM((T, HEADS), F32), sems, sems, two, pltpu.SemaphoreType.DMA((3,)),
        ],
    )
    recv = exchanged(sent.reshape(PEERS, 1, SPAN * E)).reshape(PEERS * SPAN, E)
    weights, mixed_part, query_dec = call(
        local_kernel, [((HEADS, T, T), BF16), (wide, F32), (wide, BF16)],
        q, k, v, run_row, run_col, flops=4 * HEADS * T * T * E, hbm_in=(0, 1, 2), hbm_out=(0,),
        scratch=[narrow, narrow, narrow, square, sems, sems, sems, sems],
    )
    recv, mixed_part, query_dec = lax.optimization_barrier((recv, mixed_part, query_dec))
    total, decays = call(
        group_total_kernel, [((ROWS + 8, E), F32), ((PEERS, E), F32)], recv,
    )
    other = swapped(total)
    both = both_of(False, ROWS + 8, total, other, total, other)
    far3, far2, far1 = [shifted(both, by) for by in (3, 2, 1)]
    entering = exchanged(spread(False, recv, decays, far3, far2, far1, other, far3, far2, far1, other))
    entering = entering.reshape(HEADS, E, E)

    attended, grad_mixed, state, half = call(
        mixed_kernel, [(wide, BF16), (wide, BF16), ((HEADS, E, E), F32), ((HEADS, E, E), BF16)],
        mixed_part, query_dec, g, entering, flops=4 * HEADS * T * E * E, hbm_out=(2, 3),
        scratch=[pltpu.VMEM((HEADS, E, E), F32), pltpu.VMEM((HEADS, E, E), BF16), two, two],
    )
    recv = exchanged(state.reshape(PEERS, ROWS, E)).reshape(PEERS * ROWS, E)
    grad_q, part_k, part_v, attended = call(
        local_grads_kernel, [(wide, BF16), (wide, F32), (wide, F32), (wide, BF16)],
        q, k, v, weights, run_row, run_col, grad_mixed, half, attended, flops=9 * HEADS * T * T * E,
        hbm_in=(0, 1, 2, 3), hbm_out=(0, 3),
        scratch=[narrow, narrow, narrow, square, narrow, sems, sems, sems, sems, sems, sems],
    )
    recv, part_k, part_v = lax.optimization_barrier((recv, part_k, part_v))
    back_total = call(back_total_kernel, [((ROWS, E), F32)], recv, decays)[0]
    back_other = swapped(back_total)
    back_both = both_of(True, ROWS, back_total, back_other, total, other)
    back3, back2, back1 = [shifted(back_both, -by) for by in (3, 2, 1)]
    leaving = exchanged(spread(True, recv, decays, back3, back2, back1, back_other, far1, far2, far3, other))
    leaving = leaving.reshape(HEADS, E, E)
    grad_k, grad_v = call(
        final_kernel, [(wide, BF16), (wide, BF16)],
        k, v, run_col, part_k, part_v, leaving, flops=4 * HEADS * T * E * E, hbm_in=(4,), hbm_out=(0, 1),
        scratch=[pltpu.VMEM(wide, F32), narrow, narrow, two, sems, two],
    )
    return attended, grad_q, grad_k, grad_v


def solution(mesh):
    finer = Mesh(mesh.devices.reshape(4, 2, 4, 8), ALL)
    rows = P(ALL, None)
    return jax.shard_map(
        body,
        mesh=finer,
        in_specs=(rows, rows, rows, P(None, ALL), rows),
        out_specs=(rows, rows, rows, rows),
        check_vma=False,
    )
```

```python
import math

import jax
import jax.numpy as jnp
from jax import lax
from jax.experimental import pallas as pl
from jax.experimental.pallas import tpu as pltpu
from jax.sharding import Mesh
from jax.sharding import PartitionSpec as P

ALL = ("y", "core", "x", "z")
GROUP = ("x", "z")
EPSILON = 1e-06
HEADS = 8
E = 128
T = 256
PEERS = 32
ROWS = HEADS * E // PEERS
PER_HEAD = PEERS // HEADS
SPAN = ROWS + 1
PIECES = 1
SCALING = 1.0 / math.sqrt(E)
F32 = jnp.float32
BF16 = jnp.bfloat16


def dot(a, b, dims, precision=None):
    return lax.dot_general(a, b, (dims, ((), ())), precision=precision, preferred_element_type=F32)


NN, NT, TN = ((1,), (0,)), ((1,), (1,)), ((0,), (0,))


def lanes(h):
    return slice(h * E, (h + 1) * E)


def causal():
    t = lax.broadcasted_iota(jnp.int32, (T, T), 0)
    s = lax.broadcasted_iota(jnp.int32, (T, T), 1)
    return s <= t


def call(kernel, outs, *args, smem=0, flops=0, hbm_in=(), hbm_out=(), scratch=(), grant=16):
    def spec(space):
        return pl.BlockSpec(memory_space=space)

    ins = [spec(pltpu.SMEM if i < smem else pltpu.HBM if i in hbm_in else pltpu.VMEM) for i in range(len(args))]
    moved = sum(a.size * a.dtype.itemsize for a in args)
    moved += sum(math.prod(s) * jnp.dtype(d).itemsize for s, d in outs)
    return pl.pallas_call(
        kernel,
        out_shape=[pltpu.HBM(s, d) if i in hbm_out else jax.ShapeDtypeStruct(s, d) for i, (s, d) in enumerate(outs)],
        in_specs=ins,
        out_specs=[spec(pltpu.HBM if i in hbm_out else pltpu.VMEM) for i in range(len(outs))],
        scratch_shapes=scratch,
        cost_estimate=pl.CostEstimate(flops=flops, bytes_accessed=moved, transcendentals=0),
        compiler_params=pltpu.CompilerParams(vmem_limit_bytes=grant * 1024 * 1024),
    )(*[pltpu.with_memory_space_constraint(a, pltpu.HBM) if i in hbm_in else a for i, a in enumerate(args)])


def pieces(source, target, sems, count=PIECES):
    size = source.shape[0] // count
    return [
        pltpu.make_async_copy(source.at[pl.ds(i * size, size)], target.at[pl.ds(i * size, size)], sems.at[i])
        for i in range(count)
    ]


def start(copies):
    for copy in copies:
        copy.start()


def wait(copies):
    for copy in copies:
        copy.wait()


def half_copies(pairs, half, wide):
    copies = []
    for source, target, sem in pairs:
        if wide:
            here = pl.ds(half * HEADS * E // 2, HEADS * E // 2)
            copies.append(pltpu.make_async_copy(source.at[:, here], target.at[:, here], sem.at[half]))
        else:
            size = source.shape[0] // 2
            here = pl.ds(half * size, size)
            copies.append(pltpu.make_async_copy(source.at[here], target.at[here], sem.at[half]))
    return copies


def states_kernel(
    k_hbm, v_hbm, decay_hbm, sent_hbm, run_row_ref, run_col_ref,
    k_ref, v_ref, decay_ref, sent_ref, k_sem, v_sem, out_sem, small_sem,
):
    load_decay = pltpu.make_async_copy(decay_hbm, decay_ref, small_sem.at[0])
    loads = pieces(k_hbm, k_ref, k_sem) + pieces(v_hbm, v_ref, v_sem)
    load_decay.start()
    start(loads)
    ones = jnp.where(causal(), 1.0, 0.0).astype(F32)
    load_decay.wait()
    decay = decay_ref[...]
    run_row = dot(decay, ones, NT, lax.Precision.HIGHEST)
    run_col = dot(ones, decay, NT, lax.Precision.HIGHEST)
    run_row_ref[...] = run_row
    run_col_ref[...] = run_col
    totals = jnp.broadcast_to(run_row[:, T - 1 : T], (HEADS, E))
    shrink = jnp.exp(run_col[T - 1 : T, :] - run_col)
    wait(loads)
    for half in range(2):
        for h in range(half * HEADS // 2, (half + 1) * HEADS // 2):
            key_dec = (k_ref[:, lanes(h)].astype(F32) * shrink[:, h : h + 1]).astype(BF16)
            state = dot(key_dec, v_ref[:, lanes(h)], TN)
            for i in range(PER_HEAD):
                row = (h * PER_HEAD + i) * SPAN
                sent_ref[row : row + ROWS] = state[i * ROWS : (i + 1) * ROWS]
                sent_ref[row + ROWS : row + SPAN] = totals[h : h + 1]
        start(half_copies([(sent_ref, sent_hbm, out_sem)], half, False))
    for half in range(2):
        wait(half_copies([(sent_ref, sent_hbm, out_sem)], half, False))


def local_kernel(
    q_hbm, k_hbm, v_hbm, run_row_ref, run_col_ref, weights_hbm, mixed_ref, query_dec_ref,
    q_ref, k_ref, v_ref, weights_ref, q_sem, k_sem, v_sem, out_sem,
):
    loads = pieces(q_hbm, q_ref, q_sem) + pieces(k_hbm, k_ref, k_sem) + pieces(v_hbm, v_ref, v_sem)
    start(loads)
    mask = causal()
    growth = jnp.exp(run_col_ref[...])
    wait(loads)
    for h in range(HEADS):
        q = q_ref[:, lanes(h)]
        gap = run_col_ref[:, h : h + 1] - run_row_ref[h : h + 1, :]
        decay = jnp.exp(jnp.where(mask, gap, -1e30))
        scores = dot(q, k_ref[:, lanes(h)], NT)
        weights = (scores * SCALING * decay).astype(BF16)
        weights_ref[h] = weights
        mixed_ref[:, lanes(h)] = dot(weights, v_ref[:, lanes(h)], NN)
        query_dec_ref[:, lanes(h)] = (q.astype(F32) * growth[:, h : h + 1]).astype(BF16)
    stores = pieces(weights_ref, weights_hbm, out_sem)
    start(stores)
    wait(stores)


def mixed_kernel(
    mixed_ref, query_dec_ref, g_ref, entering_ref, attended_ref, grad_mixed_ref, state_hbm, half_hbm,
    state_ref, half_ref, state_sem, half_sem,
):
    def send(half):
        return half_copies([(state_ref, state_hbm, state_sem), (half_ref, half_hbm, half_sem)], half, False)

    for half in range(2):
        for h in range(half * HEADS // 2, (half + 1) * HEADS // 2):
            query_dec = query_dec_ref[:, lanes(h)]
            entering = entering_ref[h].astype(BF16)
            half_ref[h] = entering
            mixed = mixed_ref[:, lanes(h)] + SCALING * dot(query_dec, entering, NN)
            inverse = lax.rsqrt(jnp.mean(mixed * mixed, axis=1, keepdims=True) + EPSILON)
            normed = mixed * inverse
            attended_ref[:, lanes(h)] = normed.astype(BF16)
            g = g_ref[:, lanes(h)].astype(F32)
            grad_mixed = inverse * (g - normed * jnp.mean(g * normed, axis=1, keepdims=True))
            grad_mixed = grad_mixed.astype(BF16)
            grad_mixed_ref[:, lanes(h)] = grad_mixed
            state_ref[h] = SCALING * dot(query_dec, grad_mixed, TN)
        start(send(half))
    for half in range(2):
        wait(send(half))


def local_grads_kernel(
    q_hbm, k_hbm, v_hbm, weights_hbm, run_row_ref, run_col_ref, grad_mixed_ref, half_ref, attended_ref,
    grad_q_hbm, part_k_ref, part_v_ref, attended_hbm,
    q_ref, k_ref, v_ref, weights_ref, grad_q_ref, q_sem, k_sem, v_sem, w_sem, out_sem, attended_sem,
):
    store_attended = pieces(attended_ref, attended_hbm, attended_sem)
    start(store_attended)
    loads = pieces(q_hbm, q_ref, q_sem) + pieces(k_hbm, k_ref, k_sem)
    loads += pieces(v_hbm, v_ref, v_sem) + pieces(weights_hbm, weights_ref, w_sem)
    start(loads)
    mask = causal()
    growth = jnp.exp(run_col_ref[...]) * SCALING
    wait(loads)
    for h in range(HEADS):
        grad_mixed = grad_mixed_ref[:, lanes(h)]
        gap = run_col_ref[:, h : h + 1] - run_row_ref[h : h + 1, :]
        decay = jnp.exp(jnp.where(mask, gap, -1e30))
        grad_prob = dot(grad_mixed, v_ref[:, lanes(h)], NT)
        grad_score = (grad_prob * SCALING * decay).astype(BF16)
        grad_q = dot(grad_score, k_ref[:, lanes(h)], NN)
        grad_q = grad_q + growth[:, h : h + 1] * dot(grad_mixed, half_ref[h], NT)
        grad_q_ref[:, lanes(h)] = grad_q.astype(BF16)
        part_k_ref[:, lanes(h)] = dot(grad_score, q_ref[:, lanes(h)], TN)
        part_v_ref[:, lanes(h)] = dot(weights_ref[h], grad_mixed, TN)
    stores = pieces(grad_q_ref, grad_q_hbm, out_sem)
    start(stores)
    wait(stores + store_attended)


def final_kernel(
    k_ref, v_ref, run_col_ref, part_k_ref, part_v_hbm, leaving_ref, grad_k_hbm, grad_v_hbm,
    part_v_ref, grad_k_ref, grad_v_ref, in_sem, k_sem, v_sem,
):
    loads = [half_copies([(part_v_hbm, part_v_ref, in_sem)], half, True) for half in range(2)]
    start(loads[0] + loads[1])
    run_col = run_col_ref[...]
    shrink = jnp.exp(run_col[T - 1 : T, :] - run_col)
    for h in range(HEADS):
        grad_k = shrink[:, h : h + 1] * dot(v_ref[:, lanes(h)], leaving_ref[h].astype(BF16), NT)
        grad_k_ref[:, lanes(h)] = (part_k_ref[:, lanes(h)] + grad_k).astype(BF16)
    stores = pieces(grad_k_ref, grad_k_hbm, k_sem)
    start(stores)
    for half in range(2):
        wait(loads[half])
        for h in range(half * HEADS // 2, (half + 1) * HEADS // 2):
            key_dec = (k_ref[:, lanes(h)].astype(F32) * shrink[:, h : h + 1]).astype(BF16)
            grad_v = dot(key_dec, leaving_ref[h].astype(BF16), NN)
            grad_v_ref[:, lanes(h)] = (part_v_ref[:, lanes(h)] + grad_v).astype(BF16)
        store = half_copies([(grad_v_ref, grad_v_hbm, v_sem)], half, True)
        start(store)
        stores += store
    wait(stores)


def group_total_kernel(recv_ref, total_ref, decays_ref):
    total = recv_ref[:ROWS]
    logs = recv_ref[ROWS:SPAN]
    decays_ref[0:1, :] = jnp.exp(logs)
    for j in range(1, PEERS):
        log = recv_ref[j * SPAN + ROWS : (j + 1) * SPAN]
        decay = jnp.exp(log)
        decays_ref[j : j + 1, :] = decay
        total = decay * total + recv_ref[j * SPAN : j * SPAN + ROWS]
        logs = logs + log
    total_ref[:ROWS, :] = total
    total_ref[ROWS:, :] = jnp.broadcast_to(jnp.exp(logs), (8, E))


def back_total_kernel(recv_ref, decays_ref, total_ref):
    total = recv_ref[(PEERS - 1) * ROWS :]
    for j in reversed(range(PEERS - 1)):
        total = decays_ref[j : j + 1, :] * total + recv_ref[j * ROWS : (j + 1) * ROWS]
    total_ref[...] = total


def both_kernel(reverse, mine_ref, other_ref, decay_mine_ref, decay_other_ref, both_ref):
    mine, other = mine_ref[:ROWS, :], other_ref[:ROWS, :]
    decay_mine, decay_other = decay_mine_ref[ROWS : ROWS + 1, :], decay_other_ref[ROWS : ROWS + 1, :]
    core = lax.axis_index("core")
    mine_last = (core == 0) if reverse else (core == 1)
    both = jnp.where(mine_last, decay_mine * other + mine, decay_other * mine + other)
    both_ref[:ROWS, :] = both
    if not reverse:
        both_ref[ROWS:, :] = jnp.broadcast_to(decay_mine * decay_other, (8, E))


def spread_kernel(
    reverse, recv_ref, decays_ref, far3_ref, far2_ref, far1_ref, other_ref,
    decay3_ref, decay2_ref, decay1_ref, decay_other_ref, out_ref,
):
    y, core = lax.axis_index("y"), lax.axis_index("core")
    span = recv_ref.shape[0] // PEERS
    state = jnp.zeros((ROWS, E), F32)
    steps = [(far3_ref, decay3_ref, 3), (far2_ref, decay2_ref, 2), (far1_ref, decay1_ref, 1)]
    for far_ref, decay_ref, by in steps:
        counts = (y + by < 4) if reverse else (y >= by)
        stepped = decay_ref[ROWS : ROWS + 1, :] * state + far_ref[:ROWS, :]
        state = jnp.where(counts, stepped, state)
    counts = (core == 0) if reverse else (core == 1)
    state = jnp.where(counts, decay_other_ref[ROWS : ROWS + 1, :] * state + other_ref[:ROWS, :], state)
    for j in reversed(range(PEERS)) if reverse else range(PEERS):
        out_ref[j] = state
        state = decays_ref[j : j + 1, :] * state + recv_ref[j * span : j * span + ROWS]


def shifted(array, by):
    return lax.ppermute(array, "y", [(i, (i + by) % 4) for i in range(4)])


def swapped(array):
    return lax.ppermute(array, "core", [(0, 1), (1, 0)])


def exchanged(array):
    return lax.all_to_all(array, GROUP, 0, 0, tiled=True)


def both_of(reverse, rows, *args):
    return call(lambda *refs: both_kernel(reverse, *refs), [((rows, E), F32)], *args)[0]


def spread(reverse, *args):
    return call(lambda *refs: spread_kernel(reverse, *refs), [((PEERS, ROWS, E), F32)], *args)[0]


def body(q, k, v, log_decay, g):
    wide = (T, HEADS * E)
    narrow = pltpu.VMEM(wide, BF16)
    square = pltpu.VMEM((HEADS, T, T), BF16)
    sems, two = pltpu.SemaphoreType.DMA((PIECES,)), pltpu.SemaphoreType.DMA((2,))

    sent, run_row, run_col = call(
        states_kernel, [((PEERS * SPAN, E), F32), ((HEADS, T), F32), ((T, HEADS), F32)],
        k, v, log_decay, flops=2 * HEADS * T * E * E, hbm_in=(0, 1, 2), hbm_out=(0,),
        scratch=[
            narrow, narrow, pltpu.VMEM((HEADS, T), F32), pltpu.VMEM((PEERS * SPAN, E), F32),
            sems, sems, two, pltpu.SemaphoreType.DMA((1,)),
        ],
    )
    recv = exchanged(sent.reshape(PEERS, 1, SPAN * E)).reshape(PEERS * SPAN, E)
    weights, mixed_part, query_dec = call(
        local_kernel, [((HEADS, T, T), BF16), (wide, F32), (wide, BF16)],
        q, k, v, run_row, run_col, flops=4 * HEADS * T * T * E, hbm_in=(0, 1, 2), hbm_out=(0,),
        scratch=[narrow, narrow, narrow, square, sems, sems, sems, sems],
    )
    recv, mixed_part, query_dec = lax.optimization_barrier((recv, mixed_part, query_dec))
    total, decays = call(
        group_total_kernel, [((ROWS + 8, E), F32), ((PEERS, E), F32)], recv,
    )
    other = swapped(total)
    both = both_of(False, ROWS + 8, total, other, total, other)
    far3, far2, far1 = [shifted(both, by) for by in (3, 2, 1)]
    entering = exchanged(spread(False, recv, decays, far3, far2, far1, other, far3, far2, far1, other))
    entering = entering.reshape(HEADS, E, E)

    attended, grad_mixed, state, half = call(
        mixed_kernel, [(wide, BF16), (wide, BF16), ((HEADS, E, E), F32), ((HEADS, E, E), BF16)],
        mixed_part, query_dec, g, entering, flops=4 * HEADS * T * E * E, hbm_out=(2, 3),
        scratch=[pltpu.VMEM((HEADS, E, E), F32), pltpu.VMEM((HEADS, E, E), BF16), two, two],
    )
    recv = exchanged(state.reshape(PEERS, ROWS, E)).reshape(PEERS * ROWS, E)
    grad_q, part_k, part_v, attended = call(
        local_grads_kernel, [(wide, BF16), (wide, F32), (wide, F32), (wide, BF16)],
        q, k, v, weights, run_row, run_col, grad_mixed, half, attended, flops=9 * HEADS * T * T * E,
        hbm_in=(0, 1, 2, 3), hbm_out=(0, 3),
        scratch=[narrow, narrow, narrow, square, narrow, sems, sems, sems, sems, sems, sems],
    )
    recv, part_k, part_v = lax.optimization_barrier((recv, part_k, part_v))
    back_total = call(back_total_kernel, [((ROWS, E), F32)], recv, decays)[0]
    back_other = swapped(back_total)
    back_both = both_of(True, ROWS, back_total, back_other, total, other)
    back3, back2, back1 = [shifted(back_both, -by) for by in (3, 2, 1)]
    leaving = exchanged(spread(True, recv, decays, back3, back2, back1, back_other, far1, far2, far3, other))
    leaving = leaving.reshape(HEADS, E, E)
    grad_k, grad_v = call(
        final_kernel, [(wide, BF16), (wide, BF16)],
        k, v, run_col, part_k, part_v, leaving, flops=4 * HEADS * T * E * E, hbm_in=(4,), hbm_out=(0, 1),
        scratch=[pltpu.VMEM(wide, F32), narrow, narrow, two, sems, two],
    )
    return attended, grad_q, grad_k, grad_v


def solution(mesh):
    finer = Mesh(mesh.devices.reshape(4, 2, 4, 8), ALL)
    rows = P(ALL, None)
    return jax.shard_map(
        body,
        mesh=finer,
        in_specs=(rows, rows, rows, P(None, ALL), rows),
        out_specs=(rows, rows, rows, rows),
        check_vma=False,
    )
```
